256 devices in a mesh: space: 16 (over x_hi, z), chan: 16 (over x_lo, y, core).
Axes of the slice: x: 4 (x_hi: 2, x_lo: 2; x = x_hi * 2 + x_lo), y: 4, z: 8, core: 2. Of those that a mesh axis runs over, the one named last changes fastest.
Arguments:
- volume: bfloat16 [4, 512, 16384], P(None, ('space', 'chan')), may hold values from -6 to 6
- conv1_weight: bfloat16 [3, 3, 3, 4, 128], replicated, may hold values from -0.625 to 0.625
- conv1_bias: float32 [128], replicated, may hold values from -3 to 3
- conv2_weight: bfloat16 [3, 3, 3, 128, 128], replicated, may hold values from -0.109375 to 0.109375
- conv2_bias: float32 [128], replicated, may hold values from -3 to 3
Outputs:
- pooled: bfloat16 [128, 128, 1024], P('chan', 'space')
The draws below stay inside these ranges and needn't reach their ends.
All inputs are finite; a program needn't handle non-finite values.
Results may differ from the reference program's by a relative error of at most 0.0085.
Values may be sent and summed in bfloat16 or wider, within the bound.
No kernel may reach another device: no remote copies, remote signals or barrier semaphores. Data moves between devices by JAX's collectives and lax.ppermute only.
A program may use at most 128 MiB of HBM per device.

```python
import jax
import jax.numpy as jnp
from jax import lax

FIELDS = 4
CH = 128
SIDE = 128
DEPTH = 256
VOL_DEPTH = 512


def block_scale(own_key, extent, shards, smallest, largest):
    level = 1.0
    for dim, parts in shards:
        steps = jax.random.uniform(jax.random.fold_in(jax.random.fold_in(own_key, 6), dim), (parts,), jnp.float32, smallest / len(shards), largest / len(shards))
        level = level * jnp.repeat(jnp.exp(steps), extent[dim] // parts).reshape((-1,) + (1,) * (len(extent) - 1 - dim))
    return level


def bell_draw(own_key, dims, deviation, most, shards=(), dtype=jnp.bfloat16):
    values = deviation * jax.random.normal(own_key, dims, jnp.float32)
    if shards:
        values = values * block_scale(own_key, dims, shards, -0.22, 0.18)
    return jnp.clip(values, -most, most).astype(dtype)


def setup_inputs(seed: int = 0) -> dict:
    streams_of = jax.random.split(jax.random.key(seed), 6)
    return {
        "volume": bell_draw(streams_of[0], (FIELDS, VOL_DEPTH, SIDE * SIDE), 1.0, 6.0, ((1, 256),)),
        "conv1_weight": bell_draw(streams_of[1], (3, 3, 3, FIELDS, CH), (27 * FIELDS) ** -0.5, 0.625),
        "conv1_bias": bell_draw(streams_of[2], (CH,), 0.5, 3.0, (), jnp.float32),
        "conv2_weight": bell_draw(streams_of[3], (3, 3, 3, CH, CH), (27 * CH) ** -0.5, 0.109375),
        "conv2_bias": bell_draw(streams_of[4], (CH,), 0.5, 3.0, (), jnp.float32),
    }


def leaky_relu(value):
    return jnp.where(value > 0, value, 0.2 * value)


def reference(volume, conv1_weight, conv1_bias, conv2_weight, conv2_bias):
    numbers = ("NCDHW", "DHWIO", "NCDHW")
    half_side = SIDE // 2
    grid = volume.astype(jnp.float32).reshape(1, FIELDS, VOL_DEPTH, SIDE, SIDE)
    first_conv = lax.conv_general_dilated(grid, conv1_weight.astype(jnp.float32), (2, 2, 2), ((1, 0), (1, 0), (1, 0)), dimension_numbers=numbers, precision=lax.Precision.HIGHEST)
    first_layer = leaky_relu(first_conv[0] + conv1_bias[:, None, None, None]).astype(jnp.bfloat16)
    second_conv = lax.conv_general_dilated(first_layer.astype(jnp.float32)[None], conv2_weight.astype(jnp.float32), (1, 1, 1), ((1, 1), (1, 1), (1, 1)), dimension_numbers=numbers, precision=lax.Precision.HIGHEST)
    active = leaky_relu(second_conv[0] + conv2_bias[:, None, None, None]).astype(jnp.bfloat16)
    blocks = active.astype(jnp.float32).reshape(CH, DEPTH // 2, 2, half_side // 2, 2, half_side // 2, 2)
    pooled = jnp.mean(blocks, axis=(2, 4, 6))
    return pooled.reshape(CH, DEPTH // 2, (half_side // 2) * (half_side // 2)).astype(jnp.bfloat16)
```

```python
import functools

import jax
import jax.numpy as jnp
from jax import lax
from jax.experimental import pallas as pl
from jax.experimental.pallas import tpu as pltpu
from jax.sharding import PartitionSpec as P

SIDE = 128
AXES = ("space", "chan")
WINDOW = 72
STEPS = 17


def leaky_relu(value):
    return jnp.where(value > 0, value, 0.2 * value)


def one_hot(condition):
    return jnp.where(condition, 1.0, 0.0).astype(jnp.bfloat16)


def body(own, mate, near, far, extra, w1, b1, w2, b2, out, grid, pick, pool):
    core = lax.axis_index("chan") % 2
    pair = lax.axis_index("space") * (lax.axis_size("chan") // 2) + lax.axis_index("chan") // 2
    pairs = lax.axis_size("space") * (lax.axis_size("chan") // 2)
    upper = core == 1

    r = lax.broadcasted_iota(jnp.int32, (384, 256), 0)
    k = lax.broadcasted_iota(jnp.int32, (384, 256), 1)
    cell = r % 128
    pick[...] = one_hot(k == (cell // 64) * 128 + 2 * (cell % 64) - 1 + r // 128) * one_hot(k // 128 == cell // 64)
    r = lax.broadcasted_iota(jnp.int32, (128, 512), 0)
    k = lax.broadcasted_iota(jnp.int32, (128, 512), 1)
    pool[...] = one_hot(r == (k // 128) * 32 + (k % 64) // 2)

    bias1 = jnp.concatenate([b1[...]] * 4, axis=1)
    lane = lax.broadcasted_iota(jnp.int32, (128, 512), 1)
    cells = lax.broadcasted_iota(jnp.int32, (128, 512), 0)
    lowest = jnp.where(pair == 0, 128, 0)
    highest = jnp.where(pair == pairs - 1, 384, 512)
    plane_ok = (lane >= lowest) & (lane < highest)
    first_col = cells % 64 == 0
    last_col = cells % 64 == 63

    def first_rows(j, _):
        halves = []
        for half in range(2):
            parts = []
            for tap in range(3):
                row = 64 * core - 3 + 4 * j + tap + 2 * half
                at = jnp.clip(row, 0, SIDE - 1)
                a, b = own[at].astype(jnp.float32), mate[at].astype(jnp.float32)
                c, d = near[at].astype(jnp.float32), far[at].astype(jnp.float32)
                e = extra[jnp.clip(row - (SIDE - WINDOW) * core, 0, WINDOW - 1)].astype(jnp.float32)
                tile = [
                    jnp.where(upper, d, c),
                    jnp.where(upper, b, a),
                    jnp.where(upper, a, b),
                    jnp.where(upper, c, d),
                    jnp.concatenate([e, jnp.zeros((4, 128), jnp.float32)], axis=0),
                ]
                tile = jnp.concatenate(tile, axis=0)
                parts.append(jnp.where(row >= 0, tile, 0.0))
            parts.append(jnp.zeros((8, 128), jnp.float32))
            halves.append(jnp.concatenate(parts, axis=0))
        lines = jnp.concatenate(halves, axis=1).astype(jnp.bfloat16)
        picked = lax.dot_general(
            pick[...], lines, (((1,), (1,)), ((), ())), preferred_element_type=jnp.float32
        ).astype(jnp.bfloat16)
        patches = jnp.concatenate([picked[0:128], picked[128:256], picked[256:384]], axis=1)
        first = jnp.dot(patches, w1[...], preferred_element_type=jnp.float32)
        first = leaky_relu(first + bias1)
        index = 2 * j + cells // 64
        ok = plane_ok & (index >= jnp.where(upper, 0, 1)) & (index < jnp.where(upper, 33, 34))
        first = jnp.where(ok, first, 0.0)
        left = jnp.where(first_col, 0.0, pltpu.roll(first, 1, 0)).astype(jnp.bfloat16)
        right = jnp.where(last_col, 0.0, pltpu.roll(first, 127, 0)).astype(jnp.bfloat16)
        first = first.astype(jnp.bfloat16)
        rows = pl.ds(pl.multiple_of(j * 128, 128), 128)
        for plane in range(4):
            span = slice(plane * 128, plane * 128 + 128)
            grid[plane, rows, 0:128] = left[:, span]
            grid[plane, rows, 128:256] = first[:, span]
            grid[plane, rows, 256:384] = right[:, span]
        return 0

    lax.fori_loop(0, STEPS, first_rows, 0)

    bias2 = jnp.concatenate([b2[...]] * 2, axis=1)

    def second_rows(m, _):
        def rows_of(plane):
            return jnp.concatenate(
                [grid[plane, pl.ds(pl.multiple_of(m * 512 + tap * 64, 64), 512), :] for tap in range(3)], axis=1
            )

        both = jnp.dot(
            rows_of(1), jnp.concatenate([w2[1], w2[0]], axis=1), preferred_element_type=jnp.float32
        )
        both += jnp.dot(
            rows_of(2), jnp.concatenate([w2[2], w2[1]], axis=1), preferred_element_type=jnp.float32
        )
        low = jnp.dot(rows_of(0), w2[0], preferred_element_type=jnp.float32)
        high = jnp.dot(rows_of(3), w2[2], preferred_element_type=jnp.float32)
        both += jnp.concatenate([low, high], axis=1)
        active = leaky_relu(both + bias2).astype(jnp.bfloat16)
        sums = jnp.dot(pool[...], active, preferred_element_type=jnp.float32)
        mean = (sums[:, 0:128] + sums[:, 128:256]) * 0.125
        out[:, pl.ds(pl.multiple_of(m * 128, 128), 128)] = jnp.transpose(mean).astype(jnp.bfloat16)
        return 0

    lax.fori_loop(0, 4, second_rows, 0)


def convolve(own, mate, near, far, extra, w1, b1, w2, b2):
    vmem = pl.BlockSpec(memory_space=pltpu.VMEM)
    return pl.pallas_call(
        body,
        out_shape=jax.ShapeDtypeStruct((128, 512), jnp.bfloat16),
        in_specs=[vmem] * 9,
        out_specs=vmem,
        scratch_shapes=[
            pltpu.VMEM((4, STEPS * 128, 384), jnp.bfloat16),
            pltpu.VMEM((384, 256), jnp.bfloat16),
            pltpu.VMEM((128, 512), jnp.bfloat16),
        ],
        compiler_params=pltpu.CompilerParams(vmem_limit_bytes=40 << 20),
        cost_estimate=pl.CostEstimate(flops=12_000_000_000, bytes_accessed=4_000_000, transcendentals=0),
        name="convolve",
    )(own, mate, near, far, extra, w1, b1, w2, b2)


def spread_weights(weight):
    channels = weight.shape[4]
    taps = jnp.transpose(weight, (2, 1, 0, 3, 4)).reshape(3, 3, 12, channels)

    def pad(value, before, after):
        return jnp.pad(value, ((0, 0), (0, 0), (before, after), (0, 0)))

    planes = [
        pad(taps[:, :, 4:], 0, 32) + pad(taps[:, :, :4], 32, 4),
        pad(taps, 4, 24),
        pad(taps, 12, 16),
        pad(taps, 20, 8),
    ]
    spread = jnp.concatenate(planes, axis=3).reshape(3, 120, 4 * channels)
    return jnp.pad(spread, ((0, 0), (0, 8), (0, 0))).reshape(384, 4 * channels)


def shards(volume, conv1_weight, conv1_bias, conv2_weight, conv2_bias):
    peers = lax.axis_size("space") * lax.axis_size("chan")
    upper = lax.axis_index("chan") % 2 == 1
    own = jnp.transpose(volume.reshape(4, 2, SIDE, SIDE), (2, 1, 0, 3)).reshape(SIDE, 8, SIDE)
    near = lax.ppermute(own, AXES, [p for i in range(1, peers - 1, 2) for p in ((i, i + 1), (i + 1, i))])
    mate = lax.ppermute(own, AXES, [(i, i ^ 1) for i in range(peers)])
    part = jnp.where(upper, mate[SIDE - WINDOW :, 4:], own[:WINDOW, 4:])
    extra = lax.ppermute(part, AXES, [(i, i + 2) for i in range(peers - 2)])
    far = lax.ppermute(near, AXES, [(i, i ^ 1) for i in range(peers)])
    w1 = spread_weights(conv1_weight)
    half = convolve(
        own, mate, near, far, extra, w1, conv1_bias[None], conv2_weight.reshape(3, 1152, 128), conv2_bias[None]
    )
    moved = lax.all_to_all(half.reshape(16, 8, 512), "chan", split_axis=0, concat_axis=0, tiled=True)
    return jnp.transpose(moved.reshape(8, 2, 8, 512), (2, 0, 1, 3)).reshape(8, 8, 1024)


def solution(mesh):
    in_specs = (P(None, AXES, None), P(), P(), P(), P())
    out_specs = P("chan", "space", None)
    return jax.shard_map(shards, mesh=mesh, in_specs=in_specs, out_specs=out_specs, check_vma=False)
```

```python
import jax
import jax.numpy as jnp
import numpy as np
from jax import lax
from jax.experimental import pallas as pl
from jax.experimental.pallas import tpu as pltpu
from jax.sharding import PartitionSpec as P

SIDE = 128
AXES = ("space", "chan")
WINDOW = 67
ROWS = 36
LINE = 40
LINES = 2960


def leaky_relu(value):
    return jnp.maximum(value, 0.2 * value)


def column(place):
    return 8 * (place % 8) + place // 8


def pick_matrix():
    row, source = np.arange(384)[:, None], np.arange(256)[None, :]
    half, place = row % 128 // 64, row % 64
    wanted = 2 * column(place) - 1 + row // 128
    return (source // 128 == half) & (source % 128 == wanted)


def pool_matrix():
    pooled, cell = np.arange(128)[:, None], np.arange(512)[None, :]
    return pooled == cell // 128 * 32 + column(cell % 64) // 2


def body(below, low, high, above, w1, b1, w2, b2, pick, pool, out, lines, center, shift):
    core = lax.axis_index("chan") % 2
    pair = lax.axis_index("space") * (lax.axis_size("chan") // 2) + lax.axis_index("chan") // 2
    pairs = lax.axis_size("space") * (lax.axis_size("chan") // 2)

    lines[0:3] = jnp.zeros((3, LINE, 128), jnp.float32)
    lines[67:74] = jnp.zeros((7, LINE, 128), jnp.float32)
    span = pl.ds(3 - 3 * core, WINDOW)
    lines[span, 0:12] = jnp.where(pair == 0, 0.0, below[...].astype(jnp.float32))
    lines[span, 12:16] = jnp.zeros((WINDOW, 4, 128), jnp.float32)
    lines[span, 16:24] = low[...].astype(jnp.float32)
    lines[span, 24:32] = high[...].astype(jnp.float32)
    lines[span, 32:40] = above[...].astype(jnp.float32)
    flat = lines.reshape(LINES, 128)

    bias1 = jnp.concatenate([b1[...]] * 4, axis=1)
    sublane = lax.broadcasted_iota(jnp.int32, (8, 512), 0)

    def first_rows(step, _):
        taken = []
        for j in range(2):
            at = step * 320 + j * 160
            taken.append(
                jnp.concatenate(
                    [flat[pl.ds(pl.multiple_of(at, 16), 128)], flat[pl.ds(pl.multiple_of(at + 80, 16), 128)]], axis=1
                )
            )
        taken = jnp.concatenate(taken, axis=0).astype(jnp.bfloat16)
        picked = lax.dot_general(
            pick[...], taken, (((1,), (1,)), ((), ())), preferred_element_type=jnp.float32
        ).astype(jnp.bfloat16)
        patches = jnp.concatenate(
            [
                jnp.concatenate([picked[tap * 128 : tap * 128 + 128, j * 128 : j * 128 + 128] for tap in range(3)], axis=1)
                for j in range(2)
            ],
            axis=0,
        )
        first = jnp.dot(patches, w1[...], preferred_element_type=jnp.float32)
        first = leaky_relu(first + bias1)
        for r in range(4):
            row = first[r * 64 : r * 64 + 64]
            before = jnp.where(sublane == 0, 0.0, pltpu.roll(row[56:64], 1, 0))
            after = jnp.where(sublane == 7, 0.0, pltpu.roll(row[0:8], 7, 0))
            wide = jnp.concatenate([before, row, after], axis=0).astype(jnp.bfloat16)
            row = row.astype(jnp.bfloat16)
            index = step * 4 + r
            for plane in range(4):
                lanes = slice(plane * 128, plane * 128 + 128)
                center[plane, pl.ds(pl.multiple_of(index * 64, 64), 64), :] = row[:, lanes]
                shift[plane, pl.ds(pl.multiple_of(index * 80, 16), 80), :] = wide[:, lanes]
        return 0

    lax.fori_loop(0, ROWS // 4, first_rows, 0)

    @pl.when(core == 0)
    def _():
        center[:, 0:64, :] = jnp.zeros((4, 64, 128), jnp.bfloat16)
        shift[:, 0:80, :] = jnp.zeros((4, 80, 128), jnp.bfloat16)

    @pl.when(core == 1)
    def _():
        center[:, 33 * 64 : 34 * 64, :] = jnp.zeros((4, 64, 128), jnp.bfloat16)
        shift[:, 33 * 80 : 34 * 80, :] = jnp.zeros((4, 80, 128), jnp.bfloat16)

    @pl.when(pair == 0)
    def _():
        center[0] = jnp.zeros((ROWS * 64, 128), jnp.bfloat16)
        shift[0] = jnp.zeros((ROWS * 80, 128), jnp.bfloat16)

    @pl.when(pair == pairs - 1)
    def _():
        center[3] = jnp.zeros((ROWS * 64, 128), jnp.bfloat16)
        shift[3] = jnp.zeros((ROWS * 80, 128), jnp.bfloat16)

    bias2 = jnp.concatenate([b2[...]] * 2, axis=1)
    nothing = jnp.zeros((384, 128), jnp.bfloat16)

    def second_rows(m, _):
        def taps_of(plane, rows):
            pieces = [
                [shift[plane, pl.ds(pl.multiple_of((m * 8 + r) * 80, 16), 64), :] for r in rows],
                [center[plane, pl.ds(pl.multiple_of((m * 8 + r) * 64, 64), 64), :] for r in rows],
                [shift[plane, pl.ds(pl.multiple_of((m * 8 + r) * 80 + 16, 16), 64), :] for r in rows],
            ]
            return [jnp.concatenate(p, axis=0) for p in pieces]

        def all_taps(plane):
            return [x for tap in range(3) for x in taps_of(plane, range(tap, tap + 8))]

        both = jnp.dot(
            jnp.concatenate(all_taps(1), axis=1), jnp.concatenate([w2[1], w2[0]], axis=1), preferred_element_type=jnp.float32
        )
        both += jnp.dot(
            jnp.concatenate(all_taps(2), axis=1), jnp.concatenate([w2[2], w2[1]], axis=1), preferred_element_type=jnp.float32
        )

        def row_pairs(plane, depth_tap):
            lines_of = jnp.concatenate([x for tap in range(4) for x in taps_of(plane, range(tap, tap + 8, 2))], axis=1)
            w = [w2[depth_tap, tap * 384 : tap * 384 + 384] for tap in range(3)]
            weights = jnp.concatenate(
                [
                    jnp.concatenate(w + [nothing], axis=0),
                    jnp.concatenate([nothing] + w, axis=0),
                ],
                axis=1,
            )
            pairs_of = jnp.dot(lines_of, weights, preferred_element_type=jnp.float32)
            return jnp.concatenate(
                [pairs_of[i * 64 : i * 64 + 64, h * 128 : h * 128 + 128] for i in range(4) for h in range(2)], axis=0
            )

        both += jnp.concatenate([row_pairs(0, 0), row_pairs(3, 2)], axis=1)
        active = leaky_relu(both + bias2).astype(jnp.bfloat16)
        sums = jnp.dot(pool[...], active, preferred_element_type=jnp.float32)
        mean = (sums[:, 0:128] + sums[:, 128:256]) * 0.125
        out[:, pl.ds(pl.multiple_of(m * 128, 128), 128)] = jnp.transpose(mean).astype(jnp.bfloat16)
        return 0

    lax.fori_loop(0, 4, second_rows, 0)


def convolve(*operands):
    vmem = pl.BlockSpec(memory_space=pltpu.VMEM)
    return pl.pallas_call(
        body,
        out_shape=jax.ShapeDtypeStruct((128, 512), jnp.bfloat16),
        in_specs=[vmem] * len(operands),
        out_specs=vmem,
        scratch_shapes=[
            pltpu.VMEM((LINES // LINE, LINE, 128), jnp.float32),
            pltpu.VMEM((4, ROWS * 64, 128), jnp.bfloat16),
            pltpu.VMEM((4, ROWS * 80, 128), jnp.bfloat16),
        ],
        compiler_params=pltpu.CompilerParams(vmem_limit_bytes=40 << 20),
        cost_estimate=pl.CostEstimate(flops=12_000_000_000, bytes_accessed=4_000_000, transcendentals=0),
        name="convolve",
    )(*operands)


def spread_weights(weight):
    channels = weight.shape[4]
    taps = jnp.transpose(weight, (2, 1, 0, 3, 4)).reshape(3, 3, 12, channels)

    def pad(value, before, after):
        return jnp.pad(value, ((0, 0), (0, 0), (before, after), (0, 0)))

    planes = [
        pad(taps, 0, 28),
        pad(taps[:, :, :4], 8, 28) + pad(taps[:, :, 4:], 16, 16),
        pad(taps, 20, 8),
        pad(taps, 28, 0),
    ]
    spread = jnp.concatenate(planes, axis=3).reshape(3, 120, 4 * channels)
    return jnp.pad(spread, ((0, 0), (0, 8), (0, 0))).reshape(384, 4 * channels)


def shards(volume, conv1_weight, conv1_bias, conv2_weight, conv2_bias):
    peers = lax.axis_size("space") * lax.axis_size("chan")
    upper = lax.axis_index("chan") % 2 == 1
    own = jnp.transpose(volume.reshape(4, 2, SIDE, SIDE), (2, 1, 0, 3)).reshape(SIDE, 8, SIDE)
    mate = lax.ppermute(own, AXES, [(i, i ^ 1) for i in range(peers)])
    low = jnp.where(upper, mate[SIDE - WINDOW :], own[:WINDOW])
    high = jnp.where(upper, own[SIDE - WINDOW :], mate[:WINDOW])
    upward = jnp.concatenate([low[:, 4:], high], axis=1)
    below = lax.ppermute(upward, AXES, [(i, (i + 2) % peers) for i in range(peers)])
    above = lax.ppermute(low, AXES, [((i + 2) % peers, i) for i in range(peers)])
    half = convolve(
        below,
        low,
        high,
        above,
        spread_weights(conv1_weight),
        conv1_bias[None],
        conv2_weight.reshape(3, 1152, 128),
        conv2_bias[None],
        jnp.asarray(pick_matrix(), jnp.bfloat16),
        jnp.asarray(pool_matrix(), jnp.bfloat16),
    )
    moved = lax.all_to_all(half.reshape(16, 8, 512), "chan", split_axis=0, concat_axis=0, tiled=True)
    return jnp.transpose(moved.reshape(8, 2, 8, 512), (2, 0, 1, 3)).reshape(8, 8, 1024)


def solution(mesh):
    in_specs = (P(None, AXES, None), P(), P(), P(), P())
    out_specs = P("chan", "space", None)
    return jax.shard_map(shards, mesh=mesh, in_specs=in_specs, out_specs=out_specs, check_vma=False)
```

```python
import jax
import jax.numpy as jnp
import numpy as np
from jax import lax
from jax.experimental import pallas as pl
from jax.experimental.pallas import tpu as pltpu
from jax.sharding import PartitionSpec as P

SIDE = 128
AXES = ("space", "chan")
WINDOW = 67
ROWS = 36
LINE = 40
LINES = 2960


def leaky_relu(value):
    return jnp.maximum(value, 0.2 * value)


def column(place):
    return 8 * (place % 8) + place // 8


def pick_matrix():
    row, source = np.arange(384)[:, None], np.arange(256)[None, :]
    half, place = row % 128 // 64, row % 64
    wanted = 2 * column(place) - 1 + row // 128
    return (source // 128 == half) & (source % 128 == wanted)


def order_matrix():
    pooled, place = np.arange(256)[:, None], np.arange(256)[None, :]
    return (pooled // 32 == place // 32) & (pooled % 32 == 4 * (place % 8) + place % 32 // 8)


def body(first_swap, second_swap, low, high, w1, b1, w2, b2, pick, order, out, lines, patches, center, shift):
    sums = pltpu.ACC
    pl.run_scoped(
        lambda *accumulators: compute(
            (accumulators[:16], accumulators[16:]),
            *(first_swap, second_swap, low, high, w1, b1, w2, b2, pick, order, out, lines, patches, center, shift),
        ),
        *[sums(unit)((64, 256), jnp.float32) for unit in range(2) for _ in range(16)],
    )


def compute(
    acc, first_swap, second_swap, low, high, w1, b1, w2, b2, pick, order, out, lines, patches, center, shift
):
    core = lax.axis_index("chan") % 2
    pair = lax.axis_index("space") * (lax.axis_size("chan") // 2) + lax.axis_index("chan") // 2
    pairs = lax.axis_size("space") * (lax.axis_size("chan") // 2)
    odd = pair % 2 == 1

    lines[0:3] = jnp.zeros((3, LINE, 128), jnp.float32)
    lines[67:74] = jnp.zeros((7, LINE, 128), jnp.float32)
    span = pl.ds(3 - 3 * core, WINDOW)
    one, two = first_swap[...].astype(jnp.float32), second_swap[...].astype(jnp.float32)
    lines[span, 0:12] = jnp.where(pair == 0, 0.0, jnp.where(odd, one, two))
    lines[span, 12:16] = jnp.zeros((WINDOW, 4, 128), jnp.float32)
    lines[span, 16:24] = low[...].astype(jnp.float32)
    lines[span, 24:32] = high[...].astype(jnp.float32)
    lines[span, 32:40] = jnp.where(odd, two[:, :8], one[:, :8])
    flat = lines.reshape(LINES, 128)

    for step in range(ROWS // 4):
        unit, base = step % 2, step // 2 % 2 * 6
        taken = []
        for j in range(2):
            at = step * 320 + j * 160
            taken.append(jnp.concatenate([flat[at : at + 128], flat[at + 80 : at + 208]], axis=1))
        taken = jnp.concatenate(taken, axis=0).astype(jnp.bfloat16)
        pltpu.matmul_push_rhs(taken, step // 2 % 2, unit, transpose=True)
        for piece in range(6):
            staged = step // 2 % 2 if piece == 0 else None
            pltpu.matmul_acc_lhs(acc[unit][base + piece], pick[piece * 64 : piece * 64 + 64, :], staged)
        for piece in range(6):
            picked = pltpu.matmul_pop(acc[unit][base + piece]).astype(jnp.bfloat16)
            lanes = slice(piece // 2 * 128, piece // 2 * 128 + 128)
            for j in range(2):
                at = step * 256 + j * 128 + piece % 2 * 64
                patches[at : at + 64, lanes] = picked[:, j * 128 : j * 128 + 128]

    sublane = lax.broadcasted_iota(jnp.int32, (8, 256), 0)
    bias1 = jnp.concatenate([b1[...]] * 2, axis=1)
    for chunk in range(ROWS // 6):
        base = chunk % 2 * 6
        for unit in range(2):
            for half in range(2):
                pltpu.matmul_push_rhs(w1[half * 256 : half * 256 + 256, unit * 256 : unit * 256 + 256], half, unit)
                for r in range(6):
                    at = (chunk * 6 + r) * 64
                    if half == 0:
                        lhs = patches[at : at + 64, 0:256]
                    else:
                        lhs = patches[at : at + 64, 256:384]
                        lhs = jnp.concatenate([lhs, lhs], axis=1)
                    pltpu.matmul_acc_lhs(acc[unit][base + r], lhs, half if r == 0 else None)
        for unit in range(2):
            for r in range(6):
                index = chunk * 6 + r
                row = leaky_relu(pltpu.matmul_pop(acc[unit][base + r]) + bias1)
                before = jnp.where(sublane == 0, 0.0, pltpu.roll(row[56:64], 1, 0))
                after = jnp.where(sublane == 7, 0.0, pltpu.roll(row[0:8], 7, 0))
                wide = jnp.concatenate([before, row, after], axis=0).astype(jnp.bfloat16)
                row = row.astype(jnp.bfloat16)
                for side in range(2):
                    lanes = slice(side * 128, side * 128 + 128)
                    center[unit * 2 + side, index * 64 : index * 64 + 64, :] = row[:, lanes]
                    shift[unit * 2 + side, index * 80 : index * 80 + 80, :] = wide[:, lanes]

    @pl.when(core == 0)
    def _():
        center[:, 0:64, :] = jnp.zeros((4, 64, 128), jnp.bfloat16)
        shift[:, 0:80, :] = jnp.zeros((4, 80, 128), jnp.bfloat16)

    @pl.when(core == 1)
    def _():
        center[:, 33 * 64 : 34 * 64, :] = jnp.zeros((4, 64, 128), jnp.bfloat16)
        shift[:, 33 * 80 : 34 * 80, :] = jnp.zeros((4, 80, 128), jnp.bfloat16)

    @pl.when(pair == 0)
    def _():
        center[0] = jnp.zeros((ROWS * 64, 128), jnp.bfloat16)
        shift[0] = jnp.zeros((ROWS * 80, 128), jnp.bfloat16)

    @pl.when(pair == pairs - 1)
    def _():
        center[3] = jnp.zeros((ROWS * 64, 128), jnp.bfloat16)
        shift[3] = jnp.zeros((ROWS * 80, 128), jnp.bfloat16)

    bias2 = jnp.concatenate([b2[...]] * 2, axis=1)
    nothing = jnp.zeros((128, 128), jnp.bfloat16)

    def block(plane, row, tap):
        if tap == 1:
            return center[plane, row * 64 : row * 64 + 64, :]
        at = row * 80 + (0 if tap == 0 else 16)
        return shift[plane, at : at + 64, :]

    def weight(depth_tap, row_tap, tap):
        if not 0 <= row_tap < 3:
            return nothing
        at = (row_tap * 3 + tap) * 128
        return w2[depth_tap, at : at + 128]

    inner = [(plane, r, c) for plane in (1, 2) for r in range(3) for c in range(3)]
    outer = [(r, c) for r in range(4) for c in range(3)]
    pooled = []
    for m in range(2):
        turn = 0
        for t in range(0, 18, 2):
            rhs = jnp.concatenate(
                [
                    jnp.concatenate([weight(plane, r, c), weight(plane - 1, r, c)], axis=1)
                    for plane, r, c in inner[t : t + 2]
                ],
                axis=0,
            )
            for unit in range(2):
                pltpu.matmul_push_rhs(rhs, turn % 2, unit)
                for i in range(8):
                    row = m * 16 + unit * 8 + i
                    lhs = jnp.concatenate([block(plane, row + r, c) for plane, r, c in inner[t : t + 2]], axis=1)
                    pltpu.matmul_acc_lhs(acc[unit][i], lhs, turn % 2 if i == 0 else None)
            turn += 1
        for plane, depth_tap, base in ((0, 0, 8), (3, 2, 12)):
            for t in range(0, 12, 2):
                rhs = jnp.concatenate(
                    [
                        jnp.concatenate([weight(depth_tap, r, c), weight(depth_tap, r - 1, c)], axis=1)
                        for r, c in outer[t : t + 2]
                    ],
                    axis=0,
                )
                for unit in range(2):
                    pltpu.matmul_push_rhs(rhs, turn % 2, unit)
                    for i in range(4):
                        row = m * 16 + unit * 8 + 2 * i
                        lhs = jnp.concatenate([block(plane, row + r, c) for r, c in outer[t : t + 2]], axis=1)
                        pltpu.matmul_acc_lhs(acc[unit][base + i], lhs, turn % 2 if i == 0 else None)
                turn += 1
        for unit in range(2):
            for i in range(4):
                lower = pltpu.matmul_pop(acc[unit][8 + i])
                upper = pltpu.matmul_pop(acc[unit][12 + i])
                total = None
                for side in range(2):
                    lanes = slice(side * 128, side * 128 + 128)
                    value = pltpu.matmul_pop(acc[unit][2 * i + side])
                    value += jnp.concatenate([lower[:, lanes], upper[:, lanes]], axis=1)
                    value = leaky_relu(value + bias2).astype(jnp.bfloat16).astype(jnp.float32)
                    value = value[:, :128] + value[:, 128:]
                    total = value if total is None else total + value
                total = jnp.concatenate(
                    [total[16 * k : 16 * k + 8] + total[16 * k + 8 : 16 * k + 16] for k in range(4)], axis=0
                )
                pooled.append((total * 0.125).astype(jnp.bfloat16))

    for k in range(2):
        rhs = jnp.concatenate(pooled[k * 8 : k * 8 + 8], axis=0)
        pltpu.matmul_push_rhs(jnp.concatenate([rhs, rhs], axis=1), k % 2, k)
        for piece in range(4):
            pltpu.matmul_acc_lhs(acc[k][piece], order[piece * 64 : piece * 64 + 64, :], k % 2 if piece == 0 else None)
        for h in range(2):
            ordered = [pltpu.matmul_pop(acc[k][2 * h + piece])[:, :128] for piece in range(2)]
            at = k * 256 + h * 128
            out[:, at : at + 128] = jnp.transpose(jnp.concatenate(ordered, axis=0)).astype(jnp.bfloat16)


def convolve(*operands):
    vmem = pl.BlockSpec(memory_space=pltpu.VMEM)
    return pl.pallas_call(
        body,
        out_shape=jax.ShapeDtypeStruct((128, 512), jnp.bfloat16),
        in_specs=[vmem] * len(operands),
        out_specs=vmem,
        scratch_shapes=[
            pltpu.VMEM((LINES // LINE, LINE, 128), jnp.float32),
            pltpu.VMEM((ROWS * 64, 384), jnp.bfloat16),
            pltpu.VMEM((4, ROWS * 64, 128), jnp.bfloat16),
            pltpu.VMEM((4, ROWS * 80, 128), jnp.bfloat16),
        ],
        compiler_params=pltpu.CompilerParams(vmem_limit_bytes=40 << 20),
        cost_estimate=pl.CostEstimate(flops=12_000_000_000, bytes_accessed=4_000_000, transcendentals=0),
        name="convolve",
    )(*operands)


def spread_weights(weight):
    channels = weight.shape[4]
    taps = jnp.transpose(weight, (2, 1, 0, 3, 4)).reshape(3, 3, 12, channels)

    def pad(value, before, after):
        return jnp.pad(value, ((0, 0), (0, 0), (before, after), (0, 0)))

    planes = [
        pad(taps, 0, 28),
        pad(taps[:, :, :4], 8, 28) + pad(taps[:, :, 4:], 16, 16),
        pad(taps, 20, 8),
        pad(taps, 28, 0),
    ]
    spread = jnp.concatenate(planes, axis=3).reshape(3, 120, 4 * channels)
    return jnp.pad(spread, ((0, 1), (0, 8), (0, 0))).reshape(512, 4 * channels)


def shards(volume, conv1_weight, conv1_bias, conv2_weight, conv2_bias):
    peers = lax.axis_size("space") * lax.axis_size("chan")
    upper = lax.axis_index("chan") % 2 == 1
    own = jnp.transpose(volume.reshape(4, 2, SIDE, SIDE), (2, 1, 0, 3)).reshape(SIDE, 8, SIDE)
    mate = lax.ppermute(own, AXES, [(i, i ^ 1) for i in range(peers)])
    low = jnp.where(upper, mate[SIDE - WINDOW :], own[:WINDOW])
    high = jnp.where(upper, own[SIDE - WINDOW :], mate[:WINDOW])
    upward = jnp.concatenate([low[:, 4:], high], axis=1)
    downward = jnp.pad(low, ((0, 0), (0, 4), (0, 0)))
    odd = lax.axis_index("chan") // 2 % 2 == 1
    ends = (0, 1, peers - 2, peers - 1)
    first_swap = lax.ppermute(jnp.where(odd, downward, upward), AXES, [(i, i ^ 2) for i in range(peers)])
    second_swap = lax.ppermute(
        jnp.where(odd, upward, downward),
        AXES,
        [(i, i ^ 1) if i in ends else (i, i + 2 if i // 2 % 2 else i - 2) for i in range(peers)],
    )
    half = convolve(
        first_swap,
        second_swap,
        low,
        high,
        spread_weights(conv1_weight),
        conv1_bias[None],
        conv2_weight.reshape(3, 1152, 128),
        conv2_bias[None],
        jnp.asarray(pick_matrix(), jnp.bfloat16),
        jnp.asarray(order_matrix(), jnp.bfloat16),
    )
    moved = lax.all_to_all(half.reshape(16, 8, 512), "chan", split_axis=0, concat_axis=0, tiled=True)
    return jnp.transpose(moved.reshape(8, 2, 8, 512), (2, 0, 1, 3)).reshape(8, 8, 1024)


def solution(mesh):
    in_specs = (P(None, AXES, None), P(), P(), P(), P())
    out_specs = P("chan", "space", None)
    function = jax.shard_map(shards, mesh=mesh, in_specs=in_specs, out_specs=out_specs, check_vma=False)
    return function
```

```python
import jax
import jax.numpy as jnp
import numpy as np
from jax import lax
from jax.experimental import pallas as pl
from jax.experimental.pallas import tpu as pltpu
from jax.sharding import PartitionSpec as P

SIDE = 128
AXES = ("space", "chan")
WINDOW = 67
ROWS = 36
LINE = 40
LINES = 2960
SPLIT = 2


def leaky_relu(value):
    return jnp.maximum(value, 0.2 * value)


def column(place):
    return 8 * (place % 8) + place // 8


def pick_matrix():
    row, source = np.arange(384)[:, None], np.arange(256)[None, :]
    half, place = row % 128 // 64, row % 64
    wanted = 2 * column(place) - 1 + row // 128
    return (source // 128 == half) & (source % 128 == wanted)


def order_matrix():
    pooled, place = np.arange(256)[:, None], np.arange(256)[None, :]
    return (pooled // 32 == place // 32) & (pooled % 32 == 4 * (place % 8) + place % 32 // 8)


def body(first_swap, second_swap, low, high, w1, w2, bias, pick, order, out, lines, patches, center, shift, edges):
    sums = pltpu.ACC
    pl.run_scoped(
        lambda *accumulators: compute(
            (accumulators[:16], accumulators[16:]),
            *(first_swap, second_swap, low, high, w1, w2, bias, pick, order, out, lines, patches, center, shift, edges),
        ),
        *[sums(unit)((64, 256), jnp.float32) for unit in range(2) for _ in range(16)],
    )


def compute(
    acc, first_swap, second_swap, low, high, w1, w2, bias, pick, order, out, lines, patches, center, shift, edges
):
    core = lax.axis_index("chan") % 2
    pair = lax.axis_index("space") * (lax.axis_size("chan") // 2) + lax.axis_index("chan") // 2
    pairs = lax.axis_size("space") * (lax.axis_size("chan") // 2)
    odd = pair % 2 == 1

    lines[0:3] = jnp.zeros((3, LINE, 128), jnp.float32)
    lines[67:74] = jnp.zeros((7, LINE, 128), jnp.float32)
    span = pl.ds(3 - 3 * core, WINDOW)
    one, two = first_swap[...].astype(jnp.float32), second_swap[...].astype(jnp.float32)
    below = jnp.where(pair == 0, 0.0, jnp.where(odd, one, two))
    above = jnp.where(odd, two[:2], one[:2])
    for plane in range(3):
        lines[span, plane * 4 : plane * 4 + 4] = below[plane]
    lines[span, 12:16] = jnp.zeros((WINDOW, 4, 128), jnp.float32)
    lines[span, 16:24] = low[...].astype(jnp.float32)
    lines[span, 24:32] = high[...].astype(jnp.float32)
    for plane in range(2):
        lines[span, 32 + plane * 4 : 36 + plane * 4] = above[plane]
    flat = lines.reshape(LINES, 128)

    for step in range(ROWS // 4):
        unit, base = step % 2, step // 2 % 2 * 6
        taken = []
        for half in range(2):
            starts = [step * 320 + half * 80, step * 320 + half * 80 + 160]
            taken.append(
                jnp.concatenate([jnp.transpose(flat[at : at + 128].astype(jnp.bfloat16)) for at in starts], axis=1)
            )
        pltpu.matmul_push_rhs(jnp.concatenate(taken, axis=0), step // 2 % 2, unit)
        for piece in range(6):
            staged = step // 2 % 2 if piece == 0 else None
            pltpu.matmul_acc_lhs(acc[unit][base + piece], pick[piece * 64 : piece * 64 + 64, :], staged)
        for piece in range(6):
            picked = pltpu.matmul_pop(acc[unit][base + piece]).astype(jnp.bfloat16)
            lanes = slice(piece // 2 * 128, piece // 2 * 128 + 128)
            for j in range(2):
                at = step * 256 + j * 128 + piece % 2 * 64
                patches[at : at + 64, lanes] = picked[:, j * 128 : j * 128 + 128]

    sublane = lax.broadcasted_iota(jnp.int32, (8, 256), 0)
    bias1 = jnp.concatenate([bias[0:1]] * 2, axis=1)
    for chunk in range(ROWS // 6):
        base = chunk % 2 * 6
        for unit in range(2):
            for half in range(2):
                pltpu.matmul_push_rhs(w1[half * 256 : half * 256 + 256, unit * 256 : unit * 256 + 256], half, unit)
                for r in range(6):
                    at = (chunk * 6 + r) * 64
                    if half == 0:
                        lhs = patches[at : at + 64, 0:256]
                    else:
                        lhs = patches[at : at + 64, 256:384]
                        lhs = jnp.concatenate([lhs, lhs], axis=1)
                    pltpu.matmul_acc_lhs(acc[unit][base + r], lhs, half if r == 0 else None)
        for unit in range(2):
            for r in range(6):
                index = chunk * 6 + r
                row = leaky_relu(pltpu.matmul_pop(acc[unit][base + r]) + bias1)
                before = jnp.where(sublane == 0, 0.0, pltpu.roll(row[56:64], 1, 0))
                after = jnp.where(sublane == 7, 0.0, pltpu.roll(row[0:8], 7, 0))
                wide = jnp.concatenate([before, row, after], axis=0).astype(jnp.bfloat16)
                row = row.astype(jnp.bfloat16)
                for side in range(2):
                    lanes = slice(side * 128, side * 128 + 128)
                    center[unit * 2 + side, index * 64 : index * 64 + 64, :] = row[:, lanes]
                    shift[unit * 2 + side, index * 80 : index * 80 + 80, :] = wide[:, lanes]

    @pl.when(core == 0)
    def _():
        center[:, 0:64, :] = jnp.zeros((4, 64, 128), jnp.bfloat16)
        shift[:, 0:80, :] = jnp.zeros((4, 80, 128), jnp.bfloat16)

    @pl.when(core == 1)
    def _():
        center[:, 33 * 64 : 34 * 64, :] = jnp.zeros((4, 64, 128), jnp.bfloat16)
        shift[:, 33 * 80 : 34 * 80, :] = jnp.zeros((4, 80, 128), jnp.bfloat16)

    @pl.when(pair == 0)
    def _():
        center[0] = jnp.zeros((ROWS * 64, 128), jnp.bfloat16)
        shift[0] = jnp.zeros((ROWS * 80, 128), jnp.bfloat16)

    @pl.when(pair == pairs - 1)
    def _():
        center[3] = jnp.zeros((ROWS * 64, 128), jnp.bfloat16)
        shift[3] = jnp.zeros((ROWS * 80, 128), jnp.bfloat16)

    bias2 = jnp.concatenate([bias[1:2]] * 2, axis=1)
    nothing = jnp.zeros((128, 128), jnp.bfloat16)

    def block(plane, row, tap):
        if tap == 1:
            return center[plane, row * 64 : row * 64 + 64, :]
        at = row * 80 + (0 if tap == 0 else 16)
        return shift[plane, at : at + 64, :]

    def weight(depth_tap, row_tap, tap):
        if not 0 <= row_tap < 3:
            return nothing
        at = (row_tap * 3 + tap) * 128
        return w2[depth_tap, at : at + 128]

    inner = [(plane, r, c) for plane in (1, 2) for r in range(3) for c in range(3)]
    outer = [(r, c) for r in range(4) for c in range(3)]
    turn = 0
    for t in range(0, 12, 2):
        for unit, (plane, depth_tap) in enumerate(((0, 0), (3, 2))):
            rhs = jnp.concatenate(
                [
                    jnp.concatenate([weight(depth_tap, r, c), weight(depth_tap, r - 1, c)], axis=1)
                    for r, c in outer[t : t + 2]
                ],
                axis=0,
            )
            pltpu.matmul_push_rhs(rhs, turn % 2, unit)
            for i in range(16):
                lhs = jnp.concatenate([block(plane, 2 * i + r, c) for r, c in outer[t : t + 2]], axis=1)
                pltpu.matmul_acc_lhs(acc[unit][i], lhs, turn % 2 if i == 0 else None)
        turn += 1
    for unit in range(2):
        for i in range(16):
            value = pltpu.matmul_pop(acc[unit][i])
            for side in range(2):
                edges[2 * i + side, :, unit * 128 : unit * 128 + 128] = value[:, side * 128 : side * 128 + 128]

    pooled = {}
    for m in range(SPLIT):
        rows = 16 // SPLIT
        for t in range(0, 18, 2):
            rhs = jnp.concatenate(
                [
                    jnp.concatenate([weight(plane, r, c), weight(plane - 1, r, c)], axis=1)
                    for plane, r, c in inner[t : t + 2]
                ],
                axis=0,
            )
            for unit in range(2):
                pltpu.matmul_push_rhs(rhs, turn % 2, unit)
                for i in range(rows):
                    row = unit * 16 + m * rows + i
                    lhs = jnp.concatenate([block(plane, row + r, c) for plane, r, c in inner[t : t + 2]], axis=1)
                    pltpu.matmul_acc_lhs(acc[unit][m * rows + i], lhs, turn % 2 if i == 0 else None)
            turn += 1
        for i in range(rows // 2):
            for unit in range(2):
                total = None
                for side in range(2):
                    piece = m * rows + 2 * i + side
                    value = pltpu.matmul_pop(acc[unit][piece]) + edges[unit * 16 + piece]
                    value = leaky_relu(value + bias2).astype(jnp.bfloat16).astype(jnp.float32)
                    value = value[:, :128] + value[:, 128:]
                    total = value if total is None else total + value
                total = jnp.concatenate(
                    [total[16 * k : 16 * k + 8] + total[16 * k + 8 : 16 * k + 16] for k in range(4)], axis=0
                )
                pooled[unit * 8 + m * (rows // 2) + i] = (total * 0.125).astype(jnp.bfloat16)

    for k in range(2):
        rhs = jnp.concatenate([pooled[i] for i in range(k * 8, k * 8 + 8)], axis=0)
        pltpu.matmul_push_rhs(jnp.concatenate([rhs, rhs], axis=1), k % 2, k)
        for piece in range(4):
            pltpu.matmul_acc_lhs(acc[k][piece], order[piece * 64 : piece * 64 + 64, :], k % 2 if piece == 0 else None)
        for h in range(2):
            ordered = [pltpu.matmul_pop(acc[k][2 * h + piece])[:, :128] for piece in range(2)]
            at = k * 256 + h * 128
            out[:, at : at + 128] = jnp.transpose(jnp.concatenate(ordered, axis=0)).astype(jnp.bfloat16)


def convolve(*operands):
    vmem = pl.BlockSpec(memory_space=pltpu.VMEM)
    return pl.pallas_call(
        body,
        out_shape=jax.ShapeDtypeStruct((128, 512), jnp.bfloat16),
        in_specs=[vmem] * len(operands),
        out_specs=vmem,
        scratch_shapes=[
            pltpu.VMEM((LINES // LINE, LINE, 128), jnp.float32),
            pltpu.VMEM((ROWS * 64, 384), jnp.bfloat16),
            pltpu.VMEM((4, ROWS * 64, 128), jnp.bfloat16),
            pltpu.VMEM((4, ROWS * 80, 128), jnp.bfloat16),
            pltpu.VMEM((32, 64, 256), jnp.float32),
        ],
        compiler_params=pltpu.CompilerParams(vmem_limit_bytes=40 << 20),
        cost_estimate=pl.CostEstimate(flops=12_000_000_000, bytes_accessed=4_000_000, transcendentals=0),
        name="convolve",
    )(*operands)


def spread_weights(weight):
    channels = weight.shape[4]
    taps = jnp.transpose(weight, (2, 1, 0, 3, 4)).reshape(3, 3, 12, channels)

    def pad(value, before, after):
        return jnp.pad(value, ((0, 0), (0, 0), (before, after), (0, 0)))

    planes = [
        pad(taps, 0, 28),
        pad(taps[:, :, :4], 8, 28) + pad(taps[:, :, 4:], 16, 16),
        pad(taps, 20, 8),
        pad(taps, 28, 0),
    ]
    spread = jnp.concatenate(planes, axis=3).reshape(3, 120, 4 * channels)
    return jnp.pad(spread, ((0, 1), (0, 8), (0, 0))).reshape(512, 4 * channels)


def shards(volume, conv1_weight, conv1_bias, conv2_weight, conv2_bias):
    peers = lax.axis_size("space") * lax.axis_size("chan")
    upper = lax.axis_index("chan") % 2 == 1
    own = jnp.transpose(volume.reshape(4, 2, SIDE, SIDE), (2, 1, 0, 3)).reshape(SIDE, 8, SIDE)
    mate = lax.ppermute(own, AXES, [(i, i ^ 1) for i in range(peers)])
    low = jnp.where(upper, mate[SIDE - WINDOW :], own[:WINDOW])
    high = jnp.where(upper, own[SIDE - WINDOW :], mate[:WINDOW])
    planes = [low[:, :4], low[:, 4:], high[:, :4], high[:, 4:]]
    upward = jnp.stack(planes[1:])
    downward = jnp.stack(planes[:2] + [jnp.zeros_like(planes[0])])
    odd = lax.axis_index("chan") // 2 % 2 == 1
    ends = (0, 1, peers - 2, peers - 1)
    first_swap = lax.ppermute(jnp.where(odd, downward, upward), AXES, [(i, i ^ 2) for i in range(peers)])
    second_swap = lax.ppermute(
        jnp.where(odd, upward, downward),
        AXES,
        [(i, i ^ 1) if i in ends else (i, i + 2 if i // 2 % 2 else i - 2) for i in range(peers)],
    )
    half = convolve(
        first_swap,
        second_swap,
        low,
        high,
        spread_weights(conv1_weight),
        conv2_weight.reshape(3, 1152, 128),
        jnp.stack([conv1_bias, conv2_bias]),
        jnp.asarray(pick_matrix(), jnp.bfloat16),
        jnp.asarray(order_matrix(), jnp.bfloat16),
    )
    moved = lax.all_to_all(half.reshape(16, 8, 512), "chan", split_axis=0, concat_axis=0, tiled=True)
    return jnp.transpose(moved.reshape(8, 2, 8, 512), (2, 0, 1, 3)).reshape(8, 8, 1024)


def solution(mesh):
    in_specs = (P(None, AXES, None), P(), P(), P(), P())
    out_specs = P("chan", "space", None)
    function = jax.shard_map(shards, mesh=mesh, in_specs=in_specs, out_specs=out_specs, check_vma=False)
    return function
```

```python
import jax
import jax.numpy as jnp
import numpy as np
from jax import lax
from jax.experimental import pallas as pl
from jax.experimental.pallas import tpu as pltpu
from jax.sharding import PartitionSpec as P

SIDE = 128
AXES = ("space", "chan")
WINDOW = 67
ROWS = 36
LINE = 40
LINES = 2960
SPLIT = 2


def leaky_relu(value):
    return jnp.maximum(value, 0.2 * value)


def column(place):
    return 8 * (place % 8) + place // 8


def pick_matrix():
    row, source = np.arange(384)[:, None], np.arange(256)[None, :]
    half, place = row % 128 // 64, row % 64
    wanted = 2 * column(place) - 1 + row // 128
    return (source // 128 == half) & (source % 128 == wanted)


def order_matrix():
    pooled, place = np.arange(256)[:, None], np.arange(256)[None, :]
    return (pooled // 32 == place // 32) & (pooled % 32 == 4 * (place % 8) + place % 32 // 8)


def body(lowest, kept, given, low, high, w1, w2, bias, pick, order, out, lines, patches, center, shift, edges):
    sums = pltpu.ACC
    pl.run_scoped(
        lambda *accumulators: compute(
            (accumulators[:16], accumulators[16:]),
            *(lowest, kept, given, low, high, w1, w2, bias, pick, order, out, lines, patches, center, shift, edges),
        ),
        *[sums(unit)((64, 256), jnp.float32) for unit in range(2) for _ in range(16)],
    )


def compute(
    acc, lowest, kept, given, low, high, w1, w2, bias, pick, order, out, lines, patches, center, shift, edges
):
    core = lax.axis_index("chan") % 2
    pair = lax.axis_index("space") * (lax.axis_size("chan") // 2) + lax.axis_index("chan") // 2
    pairs = lax.axis_size("space") * (lax.axis_size("chan") // 2)
    upper = core == 1

    lines[0:3] = jnp.zeros((3, LINE, 128), jnp.float32)
    lines[67:74] = jnp.zeros((7, LINE, 128), jnp.float32)
    span = pl.ds(3 - 3 * core, WINDOW)
    mine, other = kept[...].astype(jnp.float32), given[...].astype(jnp.float32)
    lines[span, 0:8] = jnp.where(pair == 0, 0.0, jnp.where(upper, other, mine))
    lines[span, 8:12] = jnp.where(pair == 0, 0.0, lowest[...].astype(jnp.float32))
    lines[span, 12:16] = jnp.zeros((WINDOW, 4, 128), jnp.float32)
    lines[span, 16:24] = low[...].astype(jnp.float32)
    lines[span, 24:32] = high[...].astype(jnp.float32)
    lines[span, 32:40] = jnp.where(upper, mine, other)
    flat = lines.reshape(LINES, 128)

    for step in range(ROWS // 4):
        unit, base = step % 2, step // 2 % 2 * 6
        taken = []
        for half in range(2):
            starts = [step * 320 + half * 80, step * 320 + half * 80 + 160]
            taken.append(
                jnp.concatenate([jnp.transpose(flat[at : at + 128].astype(jnp.bfloat16)) for at in starts], axis=1)
            )
        pltpu.matmul_push_rhs(jnp.concatenate(taken, axis=0), step // 2 % 2, unit)
        for piece in range(6):
            staged = step // 2 % 2 if piece == 0 else None
            pltpu.matmul_acc_lhs(acc[unit][base + piece], pick[piece * 64 : piece * 64 + 64, :], staged)
        for piece in range(6):
            picked = pltpu.matmul_pop(acc[unit][base + piece]).astype(jnp.bfloat16)
            lanes = slice(piece // 2 * 128, piece // 2 * 128 + 128)
            for j in range(2):
                at = step * 256 + j * 128 + piece % 2 * 64
                patches[at : at + 64, lanes] = picked[:, j * 128 : j * 128 + 128]

    sublane = lax.broadcasted_iota(jnp.int32, (8, 256), 0)
    bias1 = jnp.concatenate([bias[0:1]] * 2, axis=1)
    for chunk in range(ROWS // 6):
        base = chunk % 2 * 6
        for unit in range(2):
            for half in range(2):
                pltpu.matmul_push_rhs(w1[half * 256 : half * 256 + 256, unit * 256 : unit * 256 + 256], half, unit)
                for r in range(6):
                    at = (chunk * 6 + r) * 64
                    if half == 0:
                        lhs = patches[at : at + 64, 0:256]
                    else:
                        lhs = patches[at : at + 64, 256:384]
                        lhs = jnp.concatenate([lhs, lhs], axis=1)
                    pltpu.matmul_acc_lhs(acc[unit][base + r], lhs, half if r == 0 else None)
        for unit in range(2):
            for r in range(6):
                index = chunk * 6 + r
                row = leaky_relu(pltpu.matmul_pop(acc[unit][base + r]) + bias1)
                before = jnp.where(sublane == 0, 0.0, pltpu.roll(row[56:64], 1, 0))
                after = jnp.where(sublane == 7, 0.0, pltpu.roll(row[0:8], 7, 0))
                wide = jnp.concatenate([before, row, after], axis=0).astype(jnp.bfloat16)
                row = row.astype(jnp.bfloat16)
                for side in range(2):
                    lanes = slice(side * 128, side * 128 + 128)
                    center[unit * 2 + side, index * 64 : index * 64 + 64, :] = row[:, lanes]
                    shift[unit * 2 + side, index * 80 : index * 80 + 80, :] = wide[:, lanes]

    @pl.when(core == 0)
    def _():
        center[:, 0:64, :] = jnp.zeros((4, 64, 128), jnp.bfloat16)
        shift[:, 0:80, :] = jnp.zeros((4, 80, 128), jnp.bfloat16)

    @pl.when(core == 1)
    def _():
        center[:, 33 * 64 : 34 * 64, :] = jnp.zeros((4, 64, 128), jnp.bfloat16)
        shift[:, 33 * 80 : 34 * 80, :] = jnp.zeros((4, 80, 128), jnp.bfloat16)

    @pl.when(pair == 0)
    def _():
        center[0] = jnp.zeros((ROWS * 64, 128), jnp.bfloat16)
        shift[0] = jnp.zeros((ROWS * 80, 128), jnp.bfloat16)

    @pl.when(pair == pairs - 1)
    def _():
        center[3] = jnp.zeros((ROWS * 64, 128), jnp.bfloat16)
        shift[3] = jnp.zeros((ROWS * 80, 128), jnp.bfloat16)

    bias2 = jnp.concatenate([bias[1:2]] * 2, axis=1)
    nothing = jnp.zeros((128, 128), jnp.bfloat16)

    def block(plane, row, tap):
        if tap == 1:
            return center[plane, row * 64 : row * 64 + 64, :]
        at = row * 80 + (0 if tap == 0 else 16)
        return shift[plane, at : at + 64, :]

    def weight(depth_tap, row_tap, tap):
        if not 0 <= row_tap < 3:
            return nothing
        at = (row_tap * 3 + tap) * 128
        return w2[depth_tap, at : at + 128]

    inner = [(plane, r, c) for plane in (1, 2) for r in range(3) for c in range(3)]
    outer = [(r, c) for r in range(4) for c in range(3)]
    turn = 0
    for t in range(0, 12, 2):
        for unit, (plane, depth_tap) in enumerate(((0, 0), (3, 2))):
            rhs = jnp.concatenate(
                [
                    jnp.concatenate([weight(depth_tap, r, c), weight(depth_tap, r - 1, c)], axis=1)
                    for r, c in outer[t : t + 2]
                ],
                axis=0,
            )
            pltpu.matmul_push_rhs(rhs, turn % 2, unit)
            for i in range(16):
                lhs = jnp.concatenate([block(plane, 2 * i + r, c) for r, c in outer[t : t + 2]], axis=1)
                pltpu.matmul_acc_lhs(acc[unit][i], lhs, turn % 2 if i == 0 else None)
        turn += 1
    for unit in range(2):
        for i in range(16):
            value = pltpu.matmul_pop(acc[unit][i])
            for side in range(2):
                edges[2 * i + side, :, unit * 128 : unit * 128 + 128] = value[:, side * 128 : side * 128 + 128]

    pooled = {}
    for m in range(SPLIT):
        rows = 16 // SPLIT
        for t in range(0, 18, 2):
            rhs = jnp.concatenate(
                [
                    jnp.concatenate([weight(plane, r, c), weight(plane - 1, r, c)], axis=1)
                    for plane, r, c in inner[t : t + 2]
                ],
                axis=0,
            )
            for unit in range(2):
                pltpu.matmul_push_rhs(rhs, turn % 2, unit)
                for i in range(rows):
                    row = unit * 16 + m * rows + i
                    lhs = jnp.concatenate([block(plane, row + r, c) for plane, r, c in inner[t : t + 2]], axis=1)
                    pltpu.matmul_acc_lhs(acc[unit][m * rows + i], lhs, turn % 2 if i == 0 else None)
            turn += 1
        for i in range(rows // 2):
            for unit in range(2):
                total = None
                for side in range(2):
                    piece = m * rows + 2 * i + side
                    value = pltpu.matmul_pop(acc[unit][piece]) + edges[unit * 16 + piece]
                    value = leaky_relu(value + bias2).astype(jnp.bfloat16).astype(jnp.float32)
                    value = value[:, :128] + value[:, 128:]
                    total = value if total is None else total + value
                total = jnp.concatenate(
                    [total[16 * k : 16 * k + 8] + total[16 * k + 8 : 16 * k + 16] for k in range(4)], axis=0
                )
                pooled[unit * 8 + m * (rows // 2) + i] = (total * 0.125).astype(jnp.bfloat16)

    for k in range(2):
        rhs = jnp.concatenate([pooled[i] for i in range(k * 8, k * 8 + 8)], axis=0)
        pltpu.matmul_push_rhs(jnp.concatenate([rhs, rhs], axis=1), k % 2, k)
        for piece in range(4):
            pltpu.matmul_acc_lhs(acc[k][piece], order[piece * 64 : piece * 64 + 64, :], k % 2 if piece == 0 else None)
        for h in range(2):
            ordered = [pltpu.matmul_pop(acc[k][2 * h + piece])[:, :128] for piece in range(2)]
            at = k * 256 + h * 128
            out[:, at : at + 128] = jnp.transpose(jnp.concatenate(ordered, axis=0)).astype(jnp.bfloat16)


def convolve(*operands):
    vmem = pl.BlockSpec(memory_space=pltpu.VMEM)
    return pl.pallas_call(
        body,
        out_shape=jax.ShapeDtypeStruct((128, 512), jnp.bfloat16),
        in_specs=[vmem] * len(operands),
        out_specs=vmem,
        scratch_shapes=[
            pltpu.VMEM((LINES // LINE, LINE, 128), jnp.float32),
            pltpu.VMEM((ROWS * 64, 384), jnp.bfloat16),
            pltpu.VMEM((4, ROWS * 64, 128), jnp.bfloat16),
            pltpu.VMEM((4, ROWS * 80, 128), jnp.bfloat16),
            pltpu.VMEM((32, 64, 256), jnp.float32),
        ],
        compiler_params=pltpu.CompilerParams(vmem_limit_bytes=40 << 20),
        cost_estimate=pl.CostEstimate(flops=12_000_000_000, bytes_accessed=4_000_000, transcendentals=0),
        name="convolve",
    )(*operands)


def spread_weights(weight):
    channels = weight.shape[4]
    taps = jnp.transpose(weight, (2, 1, 0, 3, 4)).reshape(3, 3, 12, channels)

    def pad(value, before, after):
        return jnp.pad(value, ((0, 0), (0, 0), (before, after), (0, 0)))

    planes = [
        pad(taps[:, :, :4], 8, 28) + pad(taps[:, :, 4:], 0, 32),
        pad(taps[:, :, :4], 4, 32) + pad(taps[:, :, 4:], 16, 16),
        pad(taps, 20, 8),
        pad(taps, 28, 0),
    ]
    spread = jnp.concatenate(planes, axis=3).reshape(3, 120, 4 * channels)
    return jnp.pad(spread, ((0, 1), (0, 8), (0, 0))).reshape(512, 4 * channels)


def by_rows(planes):
    return jnp.transpose(planes.reshape(4, 2, SIDE, SIDE), (2, 1, 0, 3)).reshape(SIDE, 8, SIDE)


def shards(volume, conv1_weight, conv1_bias, conv2_weight, conv2_bias):
    peers = lax.axis_size("space") * lax.axis_size("chan")
    upper = lax.axis_index("chan") % 2 == 1
    mates = [(i, i ^ 1) for i in range(peers)]
    bridges = [(i, i) if i in (0, peers - 1) else (i, i + 1 if i % 2 else i - 1) for i in range(peers)]
    across = lax.ppermute(volume, AXES, bridges)
    own = by_rows(volume)
    mate = lax.ppermute(own, AXES, mates)
    low = jnp.where(upper, mate[SIDE - WINDOW :], own[:WINDOW])
    high = jnp.where(upper, own[SIDE - WINDOW :], mate[:WINDOW])
    cut = low[:, 4:]
    lowest = lax.ppermute(cut, AXES, [(i, i + 2) for i in range(peers - 2)])
    across = by_rows(across)
    kept = jnp.where(upper, across[SIDE - WINDOW :], across[:WINDOW])
    given = lax.ppermute(jnp.where(upper, across[:WINDOW], across[SIDE - WINDOW :]), AXES, mates)
    half = convolve(
        lowest,
        kept,
        given,
        low,
        high,
        spread_weights(conv1_weight),
        conv2_weight.reshape(3, 1152, 128),
        jnp.stack([conv1_bias, conv2_bias]),
        jnp.asarray(pick_matrix(), jnp.bfloat16),
        jnp.asarray(order_matrix(), jnp.bfloat16),
    )
    moved = lax.all_to_all(half.reshape(16, 8, 512), "chan", split_axis=0, concat_axis=0, tiled=True)
    return jnp.transpose(moved.reshape(8, 2, 8, 512), (2, 0, 1, 3)).reshape(8, 8, 1024)


def solution(mesh):
    in_specs = (P(None, AXES, None), P(), P(), P(), P())
    out_specs = P("chan", "space", None)
    return jax.shard_map(shards, mesh=mesh, in_specs=in_specs, out_specs=out_specs, check_vma=False)
```

```python
import jax
import jax.numpy as jnp
import numpy as np
from jax import lax
from jax.experimental import pallas as pl
from jax.experimental.pallas import tpu as pltpu
from jax.sharding import PartitionSpec as P

SIDE = 128
AXES = ("space", "chan")
WINDOW = 67
ROWS = 34
LINE = 40
LINES = 2960
GROUP = 8
SPLIT = 2


def leaky_relu(value):
    return jnp.maximum(value, 0.2 * value)


def order_matrix():
    pooled, place = np.arange(256)[:, None], np.arange(256)[None, :]
    return (pooled // 32 == place // 32) & (pooled % 32 == 4 * (place % 8) + place % 32 // 8)


def body(first_swap, second_swap, low, high, w1, w2, bias, order, out, lines, columns, patches, center, shift, edges):
    sums = pltpu.ACC
    pl.run_scoped(
        lambda *accumulators: compute(
            (accumulators[:16], accumulators[16:]),
            *(first_swap, second_swap, low, high, w1, w2, bias, order, out, lines, columns, patches, center, shift, edges),
        ),
        *[sums(unit)((64, 256), jnp.float32) for unit in range(2) for _ in range(16)],
    )


def compute(
    acc, first_swap, second_swap, low, high, w1, w2, bias, order, out, lines, columns, patches, center, shift, edges
):
    core = lax.axis_index("chan") % 2
    pair = lax.axis_index("space") * (lax.axis_size("chan") // 2) + lax.axis_index("chan") // 2
    pairs = lax.axis_size("space") * (lax.axis_size("chan") // 2)
    odd = pair % 2 == 1

    lines[0:3] = jnp.zeros((3, LINE, 128), jnp.float32)
    lines[67:74] = jnp.zeros((7, LINE, 128), jnp.float32)
    span = pl.ds(3 - 3 * core, WINDOW)
    one, two = first_swap[...].astype(jnp.float32), second_swap[...].astype(jnp.float32)
    below = jnp.where(pair == 0, 0.0, jnp.where(odd, one, two))
    above = jnp.where(odd, two[:2], one[:2])
    for plane in range(3):
        lines[span, plane * 4 : plane * 4 + 4] = below[plane]
    lines[span, 12:16] = jnp.ones((WINDOW, 4, 128), jnp.float32)
    lines[span, 16:24] = low[...].astype(jnp.float32)
    lines[span, 24:32] = high[...].astype(jnp.float32)
    for plane in range(2):
        lines[span, 32 + plane * 4 : 36 + plane * 4] = above[plane]
    flat = lines.reshape(LINES, 128)

    def gather(i):
        turned = jnp.transpose(flat[i * 80 : i * 80 + 128].astype(jnp.bfloat16))
        columns[i * 136 : i * 136 + 8, :] = jnp.zeros((8, 128), jnp.float32)
        columns[i * 136 + 8 : i * 136 + 136, :] = turned.astype(jnp.float32)
        every = [columns[pl.ds(i * 136 + 7 + k, 8, stride=16), :] for k in range(17)]
        for tap in range(3):
            picked = jnp.concatenate([every[2 * b + tap] for b in range(8)], axis=0)
            patches[i * 64 : i * 64 + 64, tap * 128 : tap * 128 + 128] = picked.astype(jnp.bfloat16)

    sublane = lax.broadcasted_iota(jnp.int32, (8, 256), 0)

    def load(half):
        for unit in range(2):
            pltpu.matmul_push_rhs(w1[half * 256 : half * 256 + 256, unit * 256 : unit * 256 + 256], half, unit)

    def multiply(i, place, half, staged):
        if half == 0:
            lhs = patches[i * 64 : i * 64 + 64, 0:256]
        else:
            lhs = patches[i * 64 : i * 64 + 64, 256:384]
            lhs = jnp.concatenate([lhs, lhs], axis=1)
        for unit in range(2):
            pltpu.matmul_acc_lhs(acc[unit][place], lhs, staged)

    def finish(index, place):
        for unit in range(2):
            row = leaky_relu(pltpu.matmul_pop(acc[unit][place]))
            before = jnp.where(sublane == 0, 0.0, pltpu.roll(row[56:64], 1, 0))
            after = jnp.where(sublane == 7, 0.0, pltpu.roll(row[0:8], 7, 0))
            wide = jnp.concatenate([before, row, after], axis=0).astype(jnp.bfloat16)
            row = row.astype(jnp.bfloat16)
            for side in range(2):
                lanes = slice(side * 128, side * 128 + 128)
                center[unit * 2 + side, index * 64 : index * 64 + 64, :] = row[:, lanes]
                shift[unit * 2 + side, index * 80 : index * 80 + 80, :] = wide[:, lanes]

    groups = [range(i, min(i + GROUP, ROWS)) for i in range(0, ROWS, GROUP)]

    def taken(turn):
        return list(enumerate(groups[turn])) if 0 <= turn < len(groups) else []

    for turn in range(len(groups) + 2):
        for half in range(2):
            if taken(turn - 1):
                load(half)
            for n in range(GROUP):
                for place, i in taken(turn - 1)[n : n + 1]:
                    multiply(i, (turn - 1) % 2 * GROUP + place, half, half if place == 0 else None)
                if n % 2 == half:
                    for _, i in taken(turn)[n : n + 1]:
                        gather(i)
                    for place, i in taken(turn - 2)[n : n + 1]:
                        finish(i, turn % 2 * GROUP + place)

    @pl.when(core == 0)
    def _():
        center[:, 0:64, :] = jnp.zeros((4, 64, 128), jnp.bfloat16)
        shift[:, 0:80, :] = jnp.zeros((4, 80, 128), jnp.bfloat16)

    @pl.when(core == 1)
    def _():
        center[:, 33 * 64 : 34 * 64, :] = jnp.zeros((4, 64, 128), jnp.bfloat16)
        shift[:, 33 * 80 : 34 * 80, :] = jnp.zeros((4, 80, 128), jnp.bfloat16)

    @pl.when(pair == 0)
    def _():
        center[0] = jnp.zeros((ROWS * 64, 128), jnp.bfloat16)
        shift[0] = jnp.zeros((ROWS * 80, 128), jnp.bfloat16)

    @pl.when(pair == pairs - 1)
    def _():
        center[3] = jnp.zeros((ROWS * 64, 128), jnp.bfloat16)
        shift[3] = jnp.zeros((ROWS * 80, 128), jnp.bfloat16)

    bias2 = jnp.concatenate([bias[1:2]] * 2, axis=1)
    nothing = jnp.zeros((128, 128), jnp.bfloat16)

    def block(plane, row, tap):
        if tap == 1:
            return center[plane, row * 64 : row * 64 + 64, :]
        at = row * 80 + (0 if tap == 0 else 16)
        return shift[plane, at : at + 64, :]

    def weight(depth_tap, row_tap, tap):
        if not 0 <= row_tap < 3:
            return nothing
        at = (row_tap * 3 + tap) * 128
        return w2[depth_tap, at : at + 128]

    inner = [(plane, r, c) for plane in (1, 2) for r in range(3) for c in range(3)]
    outer = [(r, c) for r in range(4) for c in range(3)]
    turn = 0
    for t in range(0, 12, 2):
        for unit, (plane, depth_tap) in enumerate(((0, 0), (3, 2))):
            rhs = jnp.concatenate(
                [
                    jnp.concatenate([weight(depth_tap, r, c), weight(depth_tap, r - 1, c)], axis=1)
                    for r, c in outer[t : t + 2]
                ],
                axis=0,
            )
            pltpu.matmul_push_rhs(rhs, turn % 2, unit)
            for i in range(16):
                lhs = jnp.concatenate([block(plane, 2 * i + r, c) for r, c in outer[t : t + 2]], axis=1)
                pltpu.matmul_acc_lhs(acc[unit][i], lhs, turn % 2 if i == 0 else None)
        turn += 1
    for unit in range(2):
        for i in range(16):
            value = pltpu.matmul_pop(acc[unit][i])
            for side in range(2):
                edges[2 * i + side, :, unit * 128 : unit * 128 + 128] = value[:, side * 128 : side * 128 + 128]

    pooled = {}
    for m in range(SPLIT):
        rows = 16 // SPLIT
        for t in range(0, 18, 2):
            rhs = jnp.concatenate(
                [
                    jnp.concatenate([weight(plane, r, c), weight(plane - 1, r, c)], axis=1)
                    for plane, r, c in inner[t : t + 2]
                ],
                axis=0,
            )
            for unit in range(2):
                pltpu.matmul_push_rhs(rhs, turn % 2, unit)
                for i in range(rows):
                    row = unit * 16 + m * rows + i
                    lhs = jnp.concatenate([block(plane, row + r, c) for plane, r, c in inner[t : t + 2]], axis=1)
                    pltpu.matmul_acc_lhs(acc[unit][m * rows + i], lhs, turn % 2 if i == 0 else None)
            turn += 1
        for i in range(rows // 2):
            for unit in range(2):
                total = None
                for side in range(2):
                    piece = m * rows + 2 * i + side
                    value = pltpu.matmul_pop(acc[unit][piece]) + edges[unit * 16 + piece]
                    value = leaky_relu(value + bias2).astype(jnp.bfloat16).astype(jnp.float32)
                    value = value[:, :128] + value[:, 128:]
                    total = value if total is None else total + value
                total = jnp.concatenate(
                    [total[16 * k : 16 * k + 8] + total[16 * k + 8 : 16 * k + 16] for k in range(4)], axis=0
                )
                pooled[unit * 8 + m * (rows // 2) + i] = (total * 0.125).astype(jnp.bfloat16)

    for k in range(2):
        rhs = jnp.concatenate([pooled[i] for i in range(k * 8, k * 8 + 8)], axis=0)
        pltpu.matmul_push_rhs(jnp.concatenate([rhs, rhs], axis=1), k % 2, k)
        for piece in range(4):
            pltpu.matmul_acc_lhs(acc[k][piece], order[piece * 64 : piece * 64 + 64, :], k % 2 if piece == 0 else None)
        for h in range(2):
            ordered = [pltpu.matmul_pop(acc[k][2 * h + piece])[:, :128] for piece in range(2)]
            at = k * 256 + h * 128
            out[:, at : at + 128] = jnp.transpose(jnp.concatenate(ordered, axis=0)).astype(jnp.bfloat16)


def convolve(*operands):
    vmem = pl.BlockSpec(memory_space=pltpu.VMEM)
    return pl.pallas_call(
        body,
        out_shape=jax.ShapeDtypeStruct((128, 512), jnp.bfloat16),
        in_specs=[vmem] * len(operands),
        out_specs=vmem,
        scratch_shapes=[
            pltpu.VMEM((LINES // LINE, LINE, 128), jnp.float32),
            pltpu.VMEM((ROWS * 136, 128), jnp.float32),
            pltpu.VMEM((ROWS * 64, 384), jnp.bfloat16),
            pltpu.VMEM((4, ROWS * 64, 128), jnp.bfloat16),
            pltpu.VMEM((4, ROWS * 80, 128), jnp.bfloat16),
            pltpu.VMEM((32, 64, 256), jnp.float32),
        ],
        compiler_params=pltpu.CompilerParams(vmem_limit_bytes=40 << 20),
        cost_estimate=pl.CostEstimate(flops=12_000_000_000, bytes_accessed=4_000_000, transcendentals=0),
        name="convolve",
    )(*operands)


def spread_weights(weight, bias):
    channels = weight.shape[4]
    taps = jnp.transpose(weight, (2, 1, 0, 3, 4)).reshape(3, 3, 12, channels)

    def pad(value, before, after):
        return jnp.pad(value, ((0, 0), (0, 0), (before, after), (0, 0)))

    planes = [
        pad(taps, 0, 28),
        pad(taps[:, :, :4], 8, 28) + pad(taps[:, :, 4:], 16, 16),
        pad(taps, 20, 8),
        pad(taps, 28, 0),
    ]
    spread = jnp.concatenate(planes, axis=3).reshape(3, 120, 4 * channels)
    spread = jnp.pad(spread, ((0, 1), (0, 8), (0, 0))).reshape(512, 4 * channels)
    parts = []
    for _ in range(3):
        parts.append(lax.reduce_precision(bias, 8, 7))
        bias = bias - parts[-1]
    parts = jnp.tile(jnp.stack(parts).astype(weight.dtype), (1, 4))
    start = 128 + LINE + 12
    return spread + jnp.pad(parts, ((start, 512 - 3 - start), (0, 0)))


def shards(volume, conv1_weight, conv1_bias, conv2_weight, conv2_bias):
    peers = lax.axis_size("space") * lax.axis_size("chan")
    upper = lax.axis_index("chan") % 2 == 1
    own = jnp.transpose(volume.reshape(4, 2, SIDE, SIDE), (2, 1, 0, 3)).reshape(SIDE, 8, SIDE)
    mate = lax.ppermute(own, AXES, [(i, i ^ 1) for i in range(peers)])
    low = jnp.where(upper, mate[SIDE - WINDOW :], own[:WINDOW])
    high = jnp.where(upper, own[SIDE - WINDOW :], mate[:WINDOW])
    planes = [low[:, :4], low[:, 4:], high[:, :4], high[:, 4:]]
    upward = jnp.stack(planes[1:])
    downward = jnp.stack(planes[:2] + [jnp.zeros_like(planes[0])])
    odd = lax.axis_index("chan") // 2 % 2 == 1
    ends = (0, 1, peers - 2, peers - 1)
    first_swap = lax.ppermute(jnp.where(odd, downward, upward), AXES, [(i, i ^ 2) for i in range(peers)])
    second_swap = lax.ppermute(
        jnp.where(odd, upward, downward),
        AXES,
        [(i, i ^ 1) if i in ends else (i, i + 2 if i // 2 % 2 else i - 2) for i in range(peers)],
    )
    half = convolve(
        first_swap,
        second_swap,
        low,
        high,
        spread_weights(conv1_weight, conv1_bias),
        conv2_weight.reshape(3, 1152, 128),
        jnp.stack([conv1_bias, conv2_bias]),
        jnp.asarray(order_matrix(), jnp.bfloat16),
    )
    moved = lax.all_to_all(half.reshape(16, 8, 512), "chan", split_axis=0, concat_axis=0, tiled=True)
    return jnp.transpose(moved.reshape(8, 2, 8, 512), (2, 0, 1, 3)).reshape(8, 8, 1024)


def solution(mesh):
    in_specs = (P(None, AXES, None), P(), P(), P(), P())
    out_specs = P("chan", "space", None)
    return jax.shard_map(shards, mesh=mesh, in_specs=in_specs, out_specs=out_specs, check_vma=False)
```

```python
import jax
import jax.numpy as jnp
import numpy as np
from jax import lax
from jax.experimental import pallas as pl
from jax.experimental.pallas import tpu as pltpu
from jax.sharding import PartitionSpec as P

SIDE = 128
AXES = ("space", "chan")
WINDOW = 67
ROWS = 34
LINE = 40
LINES = 2960
GROUP = 8
SPLIT = 2


def leaky_relu(value):
    return jnp.maximum(value, 0.2 * value)


def gathered(columns, start, rows):
    columns[start : start + 8, :] = jnp.zeros((8, 128), jnp.float32)
    columns[start + 8 : start + 136, :] = jnp.transpose(rows.astype(jnp.bfloat16)).astype(jnp.float32)
    every = [columns[pl.ds(start + 7 + k, 8, stride=16), :] for k in range(17)]
    return [jnp.concatenate([every[2 * b + tap] for b in range(8)], axis=0).astype(jnp.bfloat16) for tap in range(3)]


def widened(row):
    sublane = lax.broadcasted_iota(jnp.int32, (8, row.shape[1]), 0)
    before = jnp.where(sublane == 0, 0.0, pltpu.roll(row[56:64], 1, 0))
    after = jnp.where(sublane == 7, 0.0, pltpu.roll(row[0:8], 7, 0))
    return jnp.concatenate([before, row, after], axis=0).astype(jnp.bfloat16)


def accumulators():
    return [pltpu.ACC(unit)((64, 256), jnp.float32) for unit in range(2) for _ in range(16)]


def local_body(low, high, w1, w2, bias, out, lines, columns, patches, center, shift):
    pl.run_scoped(
        lambda *acc: compute_local(
            (acc[:16], acc[16:]), low, high, w1, w2, bias, out, lines, columns, patches, center, shift
        ),
        *accumulators(),
    )


def compute_local(acc, low, high, w1, w2, bias, out, lines, columns, patches, center, shift):
    core = lax.axis_index("chan") % 2
    lines[0:3] = jnp.zeros((3, 16, 128), jnp.float32)
    lines[67:76] = jnp.zeros((9, 16, 128), jnp.float32)
    span = pl.ds(3 - 3 * core, WINDOW)
    lines[span, 0:8] = low[...].astype(jnp.float32)
    lines[span, 8:16] = high[...].astype(jnp.float32)
    flat = lines.reshape(76 * 16, 128)

    for i in range(0, ROWS, 2):
        rows = jnp.concatenate([flat[i * 32 : i * 32 + 64], flat[i * 32 + 32 : i * 32 + 96]], axis=0)
        for tap, picked in enumerate(gathered(columns, i // 2 * 136, rows)):
            patches[i * 32 : i * 32 + 64, tap * 128 : tap * 128 + 128] = picked

    bias1 = jnp.concatenate([bias[0:1]] * 2, axis=1)
    for unit, pieces in enumerate((range(0, 9), range(9, 17))):
        for half in range(2):
            pltpu.matmul_push_rhs(w1[half * 256 : half * 256 + 256, :], half, unit)
            for n, i in enumerate(pieces):
                if half == 0:
                    lhs = patches[i * 64 : i * 64 + 64, 0:256]
                else:
                    lhs = patches[i * 64 : i * 64 + 64, 256:384]
                    lhs = jnp.concatenate([lhs, lhs], axis=1)
                pltpu.matmul_acc_lhs(acc[unit][n], lhs, half if n == 0 else None)
        for n, i in enumerate(pieces):
            row = leaky_relu(pltpu.matmul_pop(acc[unit][n]) + bias1)
            wide = widened(row)
            row = row.astype(jnp.bfloat16)
            for side in range(2):
                lanes = slice(side * 128, side * 128 + 128)
                index = 2 * i + side
                center[index * 64 : index * 64 + 64, :] = row[:, lanes]
                shift[index * 80 : index * 80 + 80, :] = wide[:, lanes]

    @pl.when(core == 0)
    def _():
        center[0:64, :] = jnp.zeros((64, 128), jnp.bfloat16)
        shift[0:80, :] = jnp.zeros((80, 128), jnp.bfloat16)

    @pl.when(core == 1)
    def _():
        center[33 * 64 : 34 * 64, :] = jnp.zeros((64, 128), jnp.bfloat16)
        shift[33 * 80 : 34 * 80, :] = jnp.zeros((80, 128), jnp.bfloat16)

    bias2 = jnp.concatenate([bias[1:2]] * 2, axis=1)
    taps = [(r, c) for r in range(3) for c in range(3)]
    for t in range(0, 9, 2):
        pair_of = (taps[t : t + 2] * 2)[:2]
        rhs = [jnp.concatenate([block_of(w2, 2, r, c), block_of(w2, 1, r, c)], axis=1) for r, c in taps[t : t + 2]]
        if len(rhs) == 1:
            rhs.append(jnp.zeros((128, 256), jnp.bfloat16))
        rhs = jnp.concatenate(rhs, axis=0)
        for unit in range(2):
            pltpu.matmul_push_rhs(rhs, t // 2 % 2, unit)
            for i in range(16):
                row = unit * 16 + i
                lhs = jnp.concatenate([places_of(center, shift, row + r, c) for r, c in pair_of], axis=1)
                pltpu.matmul_acc_lhs(acc[unit][i], lhs, t // 2 % 2 if i == 0 else None)
    for i in range(16):
        for unit in range(2):
            out[unit * 16 + i] = pltpu.matmul_pop(acc[unit][i]) + bias2


def block_of(w2, depth_tap, row_tap, tap):
    if not 0 <= row_tap < 3:
        return jnp.zeros((128, 128), jnp.bfloat16)
    at = (row_tap * 3 + tap) * 128
    return w2[depth_tap, at : at + 128]


def places_of(center, shift, row, tap):
    if tap == 1:
        return center[row * 64 : row * 64 + 64, :]
    at = row * 80 + (0 if tap == 0 else 16)
    return shift[at : at + 64, :]


def order_matrix():
    pooled, place = np.arange(256)[:, None], np.arange(256)[None, :]
    return (pooled // 32 == place // 32) & (pooled % 32 == 4 * (place % 8) + place % 32 // 8)


def body(first_swap, second_swap, low, high, w1, w2, bias, order, partial, out, *scratch):
    pl.run_scoped(
        lambda *acc: compute(
            (acc[:16], acc[16:]),
            *(first_swap, second_swap, low, high, w1, w2, bias, order, partial, out),
            *scratch,
        ),
        *accumulators(),
    )


def compute(
    acc,
    first_swap,
    second_swap,
    low,
    high,
    w1,
    w2,
    bias,
    order,
    partial,
    out,
    lines,
    columns,
    patches,
    center,
    shift,
    edges,
):
    core = lax.axis_index("chan") % 2
    pair = lax.axis_index("space") * (lax.axis_size("chan") // 2) + lax.axis_index("chan") // 2
    pairs = lax.axis_size("space") * (lax.axis_size("chan") // 2)
    odd = pair % 2 == 1

    lines[0:3] = jnp.zeros((3, LINE, 128), jnp.float32)
    lines[67:74] = jnp.zeros((7, LINE, 128), jnp.float32)
    span = pl.ds(3 - 3 * core, WINDOW)
    one, two = first_swap[...].astype(jnp.float32), second_swap[...].astype(jnp.float32)
    below = jnp.where(pair == 0, 0.0, jnp.where(odd, one, two))
    above = jnp.where(odd, two[:2], one[:2])
    for plane in range(3):
        lines[span, plane * 4 : plane * 4 + 4] = below[plane]
    lines[span, 12:16] = jnp.ones((WINDOW, 4, 128), jnp.float32)
    lines[span, 16:24] = low[...].astype(jnp.float32)
    lines[span, 24:32] = high[...].astype(jnp.float32)
    for plane in range(2):
        lines[span, 32 + plane * 4 : 36 + plane * 4] = above[plane]
    flat = lines.reshape(LINES, 128)

    def gather(i):
        for tap, picked in enumerate(gathered(columns, i * 136, flat[i * 80 : i * 80 + 128])):
            patches[i * 64 : i * 64 + 64, tap * 128 : tap * 128 + 128] = picked

    bias1 = jnp.concatenate([bias[0:1]] * 2, axis=1)

    def load(half):
        for unit in range(2):
            pltpu.matmul_push_rhs(w1[half * 256 : half * 256 + 256, unit * 256 : unit * 256 + 256], half, unit)

    def multiply(i, place, half, staged):
        if half == 0:
            lhs = patches[i * 64 : i * 64 + 64, 0:256]
        else:
            lhs = patches[i * 64 : i * 64 + 64, 256:384]
            lhs = jnp.concatenate([lhs, lhs], axis=1)
        for unit in range(2):
            pltpu.matmul_acc_lhs(acc[unit][place], lhs, staged)

    def finish(index, place):
        for unit in range(2):
            row = pltpu.matmul_pop(acc[unit][place])
            if unit == 1:
                row = row[:, :128]
            row = leaky_relu(row + bias1[:, : row.shape[1]])
            wide = widened(row)
            row = row.astype(jnp.bfloat16)
            for side in range(2 - unit):
                lanes = slice(side * 128, side * 128 + 128)
                center[unit * 2 + side, index * 64 : index * 64 + 64, :] = row[:, lanes]
                shift[unit * 2 + side, index * 80 : index * 80 + 80, :] = wide[:, lanes]

    groups = [range(i, min(i + GROUP, ROWS)) for i in range(0, ROWS, GROUP)]

    def taken(turn):
        return list(enumerate(groups[turn])) if 0 <= turn < len(groups) else []

    for turn in range(len(groups) + 2):
        for half in range(2):
            if taken(turn - 1):
                load(half)
            for n in range(GROUP):
                for place, i in taken(turn - 1)[n : n + 1]:
                    multiply(i, (turn - 1) % 2 * GROUP + place, half, half if place == 0 else None)
                if n % 2 == half:
                    for _, i in taken(turn)[n : n + 1]:
                        gather(i)
                    for place, i in taken(turn - 2)[n : n + 1]:
                        finish(i, turn % 2 * GROUP + place)

    @pl.when(core == 0)
    def _():
        center[:, 0:64, :] = jnp.zeros((3, 64, 128), jnp.bfloat16)
        shift[:, 0:80, :] = jnp.zeros((3, 80, 128), jnp.bfloat16)

    @pl.when(core == 1)
    def _():
        center[:, 33 * 64 : 34 * 64, :] = jnp.zeros((3, 64, 128), jnp.bfloat16)
        shift[:, 33 * 80 : 34 * 80, :] = jnp.zeros((3, 80, 128), jnp.bfloat16)

    @pl.when(pair == 0)
    def _():
        center[0] = jnp.zeros((ROWS * 64, 128), jnp.bfloat16)
        shift[0] = jnp.zeros((ROWS * 80, 128), jnp.bfloat16)

    @pl.when(pair == pairs - 1)
    def _():
        center[2] = jnp.zeros((ROWS * 64, 128), jnp.bfloat16)
        shift[2] = jnp.zeros((ROWS * 80, 128), jnp.bfloat16)

    def block(plane, row, tap):
        return places_of(center.at[plane], shift.at[plane], row, tap)

    inner = [(r, c) for r in range(3) for c in range(3)]
    outer = [(r, c) for r in range(4) for c in range(3)]
    turn = 0
    for t in range(0, 12, 2):
        for unit, (plane, depth_tap) in enumerate(((0, 0), (2, 2))):
            rhs = jnp.concatenate(
                [
                    jnp.concatenate([block_of(w2, depth_tap, r, c), block_of(w2, depth_tap, r - 1, c)], axis=1)
                    for r, c in outer[t : t + 2]
                ],
                axis=0,
            )
            pltpu.matmul_push_rhs(rhs, turn % 2, unit)
            for i in range(16):
                lhs = jnp.concatenate([block(plane, 2 * i + r, c) for r, c in outer[t : t + 2]], axis=1)
                pltpu.matmul_acc_lhs(acc[unit][i], lhs, turn % 2 if i == 0 else None)
        turn += 1
    for unit in range(2):
        for i in range(16):
            value = pltpu.matmul_pop(acc[unit][i])
            for side in range(2):
                lanes = slice(unit * 128, unit * 128 + 128)
                edges[2 * i + side, :, lanes] = (
                    value[:, side * 128 : side * 128 + 128] + partial[2 * i + side, :, lanes]
                )

    pooled = {}
    for m in range(SPLIT):
        rows = 16 // SPLIT
        for t in range(0, 9, 2):
            pair_of = (inner[t : t + 2] * 2)[:2]
            rhs = [
                jnp.concatenate([block_of(w2, 1, r, c), block_of(w2, 0, r, c)], axis=1) for r, c in inner[t : t + 2]
            ]
            if len(rhs) == 1:
                rhs.append(jnp.zeros((128, 256), jnp.bfloat16))
            rhs = jnp.concatenate(rhs, axis=0)
            for unit in range(2):
                pltpu.matmul_push_rhs(rhs, turn % 2, unit)
                for i in range(rows):
                    row = unit * 16 + m * rows + i
                    lhs = jnp.concatenate([block(1, row + r, c) for r, c in pair_of], axis=1)
                    pltpu.matmul_acc_lhs(acc[unit][m * rows + i], lhs, turn % 2 if i == 0 else None)
            turn += 1
        for i in range(rows // 2):
            for unit in range(2):
                total = None
                for side in range(2):
                    piece = m * rows + 2 * i + side
                    value = pltpu.matmul_pop(acc[unit][piece]) + edges[unit * 16 + piece]
                    value = leaky_relu(value).astype(jnp.bfloat16).astype(jnp.float32)
                    value = value[:, :128] + value[:, 128:]
                    total = value if total is None else total + value
                total = jnp.concatenate(
                    [total[16 * k : 16 * k + 8] + total[16 * k + 8 : 16 * k + 16] for k in range(4)], axis=0
                )
                pooled[unit * 8 + m * (rows // 2) + i] = (total * 0.125).astype(jnp.bfloat16)

    for k in range(2):
        rhs = jnp.concatenate([pooled[i] for i in range(k * 8, k * 8 + 8)], axis=0)
        pltpu.matmul_push_rhs(jnp.concatenate([rhs, rhs], axis=1), k % 2, k)
        for piece in range(4):
            pltpu.matmul_acc_lhs(acc[k][piece], order[piece * 64 : piece * 64 + 64, :], k % 2 if piece == 0 else None)
        for h in range(2):
            ordered = [pltpu.matmul_pop(acc[k][2 * h + piece])[:, :128] for piece in range(2)]
            at = k * 256 + h * 128
            out[:, at : at + 128] = jnp.transpose(jnp.concatenate(ordered, axis=0)).astype(jnp.bfloat16)


def call(body, out, scratch, flops, *operands):
    vmem = pl.BlockSpec(memory_space=pltpu.VMEM)
    return pl.pallas_call(
        body,
        out_shape=jax.ShapeDtypeStruct(*out),
        in_specs=[vmem] * len(operands),
        out_specs=vmem,
        scratch_shapes=[pltpu.VMEM(*shape) for shape in scratch],
        compiler_params=pltpu.CompilerParams(vmem_limit_bytes=24 << 20),
        cost_estimate=pl.CostEstimate(flops=flops, bytes_accessed=4_000_000, transcendentals=0),
    )(*operands)


def local(*operands):
    scratch = [
        ((76, 16, 128), jnp.float32),
        ((ROWS // 2 * 136, 128), jnp.float32),
        ((ROWS * 32, 384), jnp.bfloat16),
        ((ROWS * 64, 128), jnp.bfloat16),
        ((ROWS * 80, 128), jnp.bfloat16),
    ]
    return call(local_body, ((32, 64, 256), jnp.float32), scratch, 2_000_000_000, *operands)


def convolve(*operands):
    scratch = [
        ((LINES // LINE, LINE, 128), jnp.float32),
        ((ROWS * 136, 128), jnp.float32),
        ((ROWS * 64, 384), jnp.bfloat16),
        ((3, ROWS * 64, 128), jnp.bfloat16),
        ((3, ROWS * 80, 128), jnp.bfloat16),
        ((32, 64, 256), jnp.float32),
    ]
    return call(body, ((128, 512), jnp.bfloat16), scratch, 8_000_000_000, *operands)


def spread_weights(weight):
    channels = weight.shape[4]
    taps = jnp.transpose(weight, (2, 1, 0, 3, 4)).reshape(3, 3, 12, channels)

    def pad(value, before, after):
        return jnp.pad(value, ((0, 0), (0, 0), (before, after), (0, 0)))

    planes = [
        pad(taps, 0, 28),
        pad(taps[:, :, :4], 8, 28) + pad(taps[:, :, 4:], 16, 16),
        pad(taps, 28, 0),
    ]
    spread = jnp.concatenate(planes, axis=3).reshape(3, 120, 3 * channels)
    spread = jnp.pad(spread, ((0, 1), (0, 8), (0, channels))).reshape(512, 4 * channels)
    inner = jnp.pad(pad(taps, 4, 0).reshape(3, 48, channels), ((0, 1), (0, 16), (0, 0)))
    inner = jnp.stack(
        [jnp.pad(inner, ((0, 0), (0, 0), (0, channels))), jnp.pad(inner, ((0, 0), (0, 0), (channels, 0)))], axis=1
    )
    return spread, inner.reshape(512, 2 * channels)


def shards(volume, conv1_weight, conv1_bias, conv2_weight, conv2_bias):
    peers = lax.axis_size("space") * lax.axis_size("chan")
    upper = lax.axis_index("chan") % 2 == 1
    own = jnp.transpose(volume.reshape(4, 2, SIDE, SIDE), (2, 1, 0, 3)).reshape(SIDE, 8, SIDE)
    mate = lax.ppermute(own, AXES, [(i, i ^ 1) for i in range(peers)])
    low = jnp.where(upper, mate[SIDE - WINDOW :], own[:WINDOW])
    high = jnp.where(upper, own[SIDE - WINDOW :], mate[:WINDOW])
    planes = [low[:, :4], low[:, 4:], high[:, :4], high[:, 4:]]
    upward = jnp.stack(planes[1:])
    downward = jnp.stack(planes[:2] + [jnp.zeros_like(planes[0])])
    odd = lax.axis_index("chan") // 2 % 2 == 1
    ends = (0, 1, peers - 2, peers - 1)
    first_swap = lax.ppermute(jnp.where(odd, downward, upward), AXES, [(i, i ^ 2) for i in range(peers)])
    second_swap = lax.ppermute(
        jnp.where(odd, upward, downward),
        AXES,
        [(i, i ^ 1) if i in ends else (i, i + 2 if i // 2 % 2 else i - 2) for i in range(peers)],
    )
    spread, inner = spread_weights(conv1_weight)
    w2 = conv2_weight.reshape(3, 1152, 128)
    bias = jnp.stack([conv1_bias, conv2_bias])
    partial = local(low, high, inner, w2, bias)
    half = convolve(
        *(first_swap, second_swap, low, high, spread, w2, bias),
        jnp.asarray(order_matrix(), jnp.bfloat16),
        partial,
    )
    moved = lax.all_to_all(half.reshape(16, 8, 512), "chan", split_axis=0, concat_axis=0, tiled=True)
    return jnp.transpose(moved.reshape(8, 2, 8, 512), (2, 0, 1, 3)).reshape(8, 8, 1024)


def solution(mesh):
    in_specs = (P(None, AXES, None), P(), P(), P(), P())
    out_specs = P("chan", "space", None)
    return jax.shard_map(shards, mesh=mesh, in_specs=in_specs, out_specs=out_specs, check_vma=False)
```

```python
import jax
import jax.numpy as jnp
import numpy as np
from jax import lax
from jax.experimental import pallas as pl
from jax.experimental.pallas import tpu as pltpu
from jax.sharding import PartitionSpec as P

SIDE = 128
AXES = ("space", "chan")
WINDOW = 68
ROWS = 34
LINE = 20
GROUP = 6
SPLIT = 2


def leaky_relu(value):
    return jnp.maximum(value, 0.2 * value)


def column(place):
    return 8 * (place % 8) + place // 8


def gathered(columns, start, rows):
    columns[start : start + 8, :] = jnp.zeros((8, 128), jnp.float32)
    columns[start + 8 : start + 136, :] = jnp.transpose(rows.astype(jnp.bfloat16)).astype(jnp.float32)
    every = [columns[pl.ds(start + 7 + k, 8, stride=16), :] for k in range(17)]
    return [jnp.concatenate([every[2 * b + tap] for b in range(8)], axis=0).astype(jnp.bfloat16) for tap in range(3)]


def widened(row):
    sublane = lax.broadcasted_iota(jnp.int32, (8, row.shape[1]), 0)
    before = jnp.where(sublane == 0, 0.0, pltpu.roll(row[56:64], 1, 0))
    after = jnp.where(sublane == 7, 0.0, pltpu.roll(row[0:8], 7, 0))
    return jnp.concatenate([before, row, after], axis=0).astype(jnp.bfloat16)


def accumulators():
    return [pltpu.ACC(unit)((64, 256), jnp.float32) for unit in range(2) for _ in range(16)]


def local_body(low, high, w1, w2, bias, out, patches, lines, columns, center, shift):
    pl.run_scoped(
        lambda *acc: compute_local(
            (acc[:16], acc[16:]), low, high, w1, w2, bias, out, patches, lines, columns, center, shift
        ),
        *accumulators(),
    )


def compute_local(acc, low, high, w1, w2, bias, out, patches, lines, columns, center, shift):
    core = lax.axis_index("chan") % 2
    lines[0:4] = jnp.zeros((4, 16, 128), jnp.float32)
    lines[68:76] = jnp.zeros((8, 16, 128), jnp.float32)
    span = pl.ds(4 - 4 * core, WINDOW)
    lines[span, 0:8] = low[...].astype(jnp.float32)
    lines[span, 8:16] = high[...].astype(jnp.float32)
    flat = lines.reshape(76 * 16, 128)

    for i in range(0, ROWS, 2):
        rows = jnp.concatenate([flat[i * 32 + 16 : i * 32 + 80], flat[i * 32 + 48 : i * 32 + 112]], axis=0)
        for tap, picked in enumerate(gathered(columns, i // 2 * 136, rows)):
            patches[i * 32 : i * 32 + 64, tap * 128 : tap * 128 + 128] = picked

    bias1 = jnp.concatenate([bias[0:1]] * 2, axis=1)
    for unit, pieces in enumerate((range(0, 9), range(9, 17))):
        for half in range(2):
            pltpu.matmul_push_rhs(w1[half * 256 : half * 256 + 256, :], half, unit)
            for n, i in enumerate(pieces):
                if half == 0:
                    lhs = patches[i * 64 : i * 64 + 64, 0:256]
                else:
                    lhs = patches[i * 64 : i * 64 + 64, 256:384]
                    lhs = jnp.concatenate([lhs, lhs], axis=1)
                pltpu.matmul_acc_lhs(acc[unit][n], lhs, half if n == 0 else None)
        for n, i in enumerate(pieces):
            row = leaky_relu(pltpu.matmul_pop(acc[unit][n]) + bias1)
            wide = widened(row)
            row = row.astype(jnp.bfloat16)
            for side in range(2):
                lanes = slice(side * 128, side * 128 + 128)
                index = 2 * i + side
                center[index * 64 : index * 64 + 64, :] = row[:, lanes]
                shift[index * 80 : index * 80 + 80, :] = wide[:, lanes]

    @pl.when(core == 0)
    def _():
        center[0:64, :] = jnp.zeros((64, 128), jnp.bfloat16)
        shift[0:80, :] = jnp.zeros((80, 128), jnp.bfloat16)

    @pl.when(core == 1)
    def _():
        center[33 * 64 : 34 * 64, :] = jnp.zeros((64, 128), jnp.bfloat16)
        shift[33 * 80 : 34 * 80, :] = jnp.zeros((80, 128), jnp.bfloat16)

    bias2 = jnp.concatenate([bias[1:2]] * 2, axis=1)
    taps = [(r, c) for r in range(3) for c in range(3)]
    for t in range(0, 9, 2):
        pair_of = (taps[t : t + 2] * 2)[:2]
        rhs = [jnp.concatenate([block_of(w2, 2, r, c), block_of(w2, 1, r, c)], axis=1) for r, c in taps[t : t + 2]]
        if len(rhs) == 1:
            rhs.append(jnp.zeros((128, 256), jnp.bfloat16))
        rhs = jnp.concatenate(rhs, axis=0)
        for unit in range(2):
            pltpu.matmul_push_rhs(rhs, t // 2 % 2, unit)
            for i in range(16):
                row = unit * 16 + i
                lhs = jnp.concatenate([places_of(center, shift, row + r, c) for r, c in pair_of], axis=1)
                pltpu.matmul_acc_lhs(acc[unit][i], lhs, t // 2 % 2 if i == 0 else None)
    for i in range(16):
        for unit in range(2):
            out[unit * 16 + i] = pltpu.matmul_pop(acc[unit][i]) + bias2


def block_of(w2, depth_tap, row_tap, tap):
    if not 0 <= row_tap < 3:
        return jnp.zeros((128, 128), jnp.bfloat16)
    at = (row_tap * 3 + tap) * 128
    return w2[depth_tap, at : at + 128]


def places_of(center, shift, row, tap):
    if tap == 1:
        return center[row * 64 : row * 64 + 64, :]
    at = row * 80 + (0 if tap == 0 else 16)
    return shift[at : at + 64, :]


def pool_matrix():
    pooled, cell = np.arange(64)[:, None], np.arange(256)[None, :]
    return pooled == cell // 128 * 32 + column(cell % 64) // 2


def body(first_swap, second_swap, w1, w2, bias, pool, partial, known, out, *scratch):
    pl.run_scoped(
        lambda *acc: compute(
            (acc[:16], acc[16:]),
            *(first_swap, second_swap, w1, w2, bias, pool, partial, known, out),
            *scratch,
        ),
        *accumulators(),
    )


def compute(
    acc,
    first_swap,
    second_swap,
    w1,
    w2,
    bias,
    pool,
    partial,
    known,
    out,
    lines,
    columns,
    patches,
    center,
    shift,
    edges,
    cells,
):
    core = lax.axis_index("chan") % 2
    pair = lax.axis_index("space") * (lax.axis_size("chan") // 2) + lax.axis_index("chan") // 2
    pairs = lax.axis_size("space") * (lax.axis_size("chan") // 2)
    odd = pair % 2 == 1

    for g in range(35):
        pieces = []
        for t in (2 * g, 2 * g + 1):
            at = t - 3 + 4 * core
            inside = (at >= 0) & (at < WINDOW)
            at = jnp.clip(at, 0, WINDOW - 1)
            for plane in range(5):
                if plane < 3:
                    keep = inside & (pair != 0)
                    x, y = first_swap[plane, at], second_swap[plane, at]
                else:
                    keep = inside
                    x, y = second_swap[plane - 3, at], first_swap[plane - 3, at]
                value = jnp.where(odd, x.astype(jnp.float32), y.astype(jnp.float32))
                pieces.append(jnp.where(keep, value, 0.0))
        lines[g * 40 : g * 40 + 40, :] = jnp.concatenate(pieces, axis=0)

    for i in range(0, ROWS, 2):
        rows = jnp.concatenate([lines[i * 40 : i * 40 + 64, :], lines[i * 40 + 40 : i * 40 + 104, :]], axis=0)
        for tap, picked in enumerate(gathered(columns, i // 2 * 136, rows)):
            patches[i * 32 : i * 32 + 64, tap * 128 : tap * 128 + 128] = picked

    @pl.when(core == 2)
    def _():
        columns[0:8, :] = jnp.zeros((8, 128), jnp.float32)

    def both(i, tile):
        at = slice(i * 64, i * 64 + 64)
        if tile == 0:
            return known[at, 0:256]
        if tile == 1:
            return jnp.concatenate([known[at, 256:384], patches[at, 0:128]], axis=1)
        return patches[at, 128:384]

    def arrived(i, tile):
        at = slice(i * 64, i * 64 + 64)
        if tile == 0:
            return patches[at, 0:256]
        return jnp.concatenate([patches[at, 256:384]] * 2, axis=1)

    bias1 = jnp.concatenate([bias[0:1]] * 2, axis=1)
    work = []
    for unit in range(2):
        jobs = [(1 + unit, 512 + 768 * unit, 3, both, range(i, min(i + GROUP, 17))) for i in range(0, 17, GROUP)]
        jobs += [(0, 0, 2, arrived, part) for part in ((range(0, 5), range(5, 9)), (range(9, 13), range(13, 17)))[unit]]
        work.append(jobs)
    for turn in range(len(work[0]) + 1):
        base = turn % 2 * 8
        if turn < len(work[0]):
            for unit in range(2):
                _, start, tiles, lhs_of, pairs_of_rows = work[unit][turn]
                for tile in range(tiles):
                    pltpu.matmul_push_rhs(w1[start + tile * 256 : start + tile * 256 + 256, :], tile % 2, unit)
                    for n, i in enumerate(pairs_of_rows):
                        pltpu.matmul_acc_lhs(acc[unit][base + n], lhs_of(i, tile), tile % 2 if n == 0 else None)
        if turn:
            for unit in range(2):
                plane, _, _, _, pairs_of_rows = work[unit][turn - 1]
                for n, i in enumerate(pairs_of_rows):
                    row = leaky_relu(pltpu.matmul_pop(acc[unit][8 - base + n]) + bias1)
                    wide = widened(row)
                    row = row.astype(jnp.bfloat16)
                    for side in range(2):
                        lanes = slice(side * 128, side * 128 + 128)
                        index = 2 * i + side
                        center[plane, index * 64 : index * 64 + 64, :] = row[:, lanes]
                        shift[plane, index * 80 : index * 80 + 80, :] = wide[:, lanes]

    @pl.when(core == 0)
    def _():
        center[:, 0:64, :] = jnp.zeros((3, 64, 128), jnp.bfloat16)
        shift[:, 0:80, :] = jnp.zeros((3, 80, 128), jnp.bfloat16)

    @pl.when(core == 1)
    def _():
        center[:, 33 * 64 : 34 * 64, :] = jnp.zeros((3, 64, 128), jnp.bfloat16)
        shift[:, 33 * 80 : 34 * 80, :] = jnp.zeros((3, 80, 128), jnp.bfloat16)

    def block(plane, row, tap):
        return places_of(center.at[plane], shift.at[plane], row, tap)

    inner = [(r, c) for r in range(3) for c in range(3)]
    outer = [(r, c) for r in range(4) for c in range(3)]
    turn = 0
    for t in range(0, 12, 2):
        for unit, (plane, depth_tap) in enumerate(((0, 0), (2, 2))):
            rhs = jnp.concatenate(
                [
                    jnp.concatenate([block_of(w2, depth_tap, r, c), block_of(w2, depth_tap, r - 1, c)], axis=1)
                    for r, c in outer[t : t + 2]
                ],
                axis=0,
            )
            pltpu.matmul_push_rhs(rhs, turn % 2, unit)
            for i in range(16):
                lhs = jnp.concatenate([block(plane, 2 * i + r, c) for r, c in outer[t : t + 2]], axis=1)
                pltpu.matmul_acc_lhs(acc[unit][i], lhs, turn % 2 if i == 0 else None)
        turn += 1
    for unit in range(2):
        for i in range(16):
            value = pltpu.matmul_pop(acc[unit][i])
            value = jnp.where(pair == (pairs - 1 if unit else 0), 0.0, value)
            for side in range(2):
                lanes = slice(unit * 128, unit * 128 + 128)
                edges[2 * i + side, :, lanes] = (
                    value[:, side * 128 : side * 128 + 128] + partial[2 * i + side, :, lanes]
                )

    def active(rows):
        for i in rows:
            for unit in range(2):
                value = leaky_relu(pltpu.matmul_pop(acc[unit][i]) + edges[unit * 16 + i])
                at = (unit * 16 + i) * 64
                cells[at : at + 64, :] = value.astype(jnp.bfloat16)

    def pooled(quarters):
        for k in quarters:
            for unit in range(2):
                at = (unit * 4 + k) * 256
                pltpu.matmul_push_rhs(cells[at : at + 256, :], k % 2, unit)
                pltpu.matmul_acc_lhs(acc[unit][k], pool[...], k % 2)
        for k in quarters[::2]:
            for unit in range(2):
                sums = jnp.concatenate([pltpu.matmul_pop(acc[unit][k + n]) for n in range(2)], axis=0)
                mean = (sums[:, :128] + sums[:, 128:]) * 0.125
                at = unit * 256 + k * 64
                out[:, at : at + 128] = jnp.transpose(mean).astype(jnp.bfloat16)

    for m in range(SPLIT):
        rows = 16 // SPLIT
        for t in range(0, 9, 2):
            pair_of = (inner[t : t + 2] * 2)[:2]
            rhs = [
                jnp.concatenate([block_of(w2, 1, r, c), block_of(w2, 0, r, c)], axis=1) for r, c in inner[t : t + 2]
            ]
            if len(rhs) == 1:
                rhs.append(jnp.zeros((128, 256), jnp.bfloat16))
            rhs = jnp.concatenate(rhs, axis=0)
            for unit in range(2):
                pltpu.matmul_push_rhs(rhs, turn % 2, unit)
                for i in range(rows):
                    row = unit * 16 + m * rows + i
                    lhs = jnp.concatenate([block(1, row + r, c) for r, c in pair_of], axis=1)
                    pltpu.matmul_acc_lhs(acc[unit][m * rows + i], lhs, turn % 2 if i == 0 else None)
            turn += 1
        active(range(m * rows, m * rows + rows))
    pooled(range(4))


def call(body, out, scratch, flops, *operands):
    vmem = pl.BlockSpec(memory_space=pltpu.VMEM)
    return pl.pallas_call(
        body,
        out_shape=[jax.ShapeDtypeStruct(*shape) for shape in out],
        in_specs=[vmem] * len(operands),
        out_specs=[vmem] * len(out),
        scratch_shapes=[pltpu.VMEM(*shape) for shape in scratch],
        compiler_params=pltpu.CompilerParams(vmem_limit_bytes=24 << 20),
        cost_estimate=pl.CostEstimate(flops=flops, bytes_accessed=4_000_000, transcendentals=0),
    )(*operands)


def local(*operands):
    out = [((32, 64, 256), jnp.float32), ((ROWS * 32, 384), jnp.bfloat16)]
    scratch = [
        ((76, 16, 128), jnp.float32),
        ((ROWS // 2 * 136, 128), jnp.float32),
        ((ROWS * 64, 128), jnp.bfloat16),
        ((ROWS * 80, 128), jnp.bfloat16),
    ]
    return call(local_body, out, scratch, 2_000_000_000, *operands)


def convolve(*operands):
    scratch = [
        ((35 * 2 * LINE, 128), jnp.float32),
        ((ROWS // 2 * 136, 128), jnp.float32),
        ((ROWS * 32, 384), jnp.bfloat16),
        ((3, ROWS * 64, 128), jnp.bfloat16),
        ((3, ROWS * 80, 128), jnp.bfloat16),
        ((32, 64, 256), jnp.float32),
        ((2048, 256), jnp.bfloat16),
    ]
    return call(body, [((128, 512), jnp.bfloat16)], scratch, 8_000_000_000, *operands)[0]


def spread_weights(weight):
    channels = weight.shape[4]
    taps = jnp.transpose(weight, (2, 1, 0, 3, 4)).reshape(3, 3, 12, channels)

    def paired(value, before, after):
        value = jnp.pad(value, ((0, 0), (0, 0), (before, after), (0, 0)))
        value = value.reshape(3, -1, channels)
        value = jnp.pad(value, ((0, 0), (0, 64 - value.shape[1]), (0, 0)))
        sides = [jnp.pad(value, ((0, 0), (0, 0), (0, channels))), jnp.pad(value, ((0, 0), (0, 0), (channels, 0)))]
        return jnp.stack(sides, axis=1).reshape(384, 2 * channels)

    nothing = jnp.zeros((128, 2 * channels), weight.dtype)
    inner = jnp.concatenate([paired(taps, 4, 0), nothing])
    first, rest = taps[:, :, :4], taps[:, :, 4:]
    others = [paired(taps, 0, 8), nothing]
    others += [paired(rest, 0, 8), paired(first, 8, 8)]
    others += [paired(first, 12, 0), paired(rest, 12, 0)]
    return jnp.concatenate(others), inner


def shards(volume, conv1_weight, conv1_bias, conv2_weight, conv2_bias):
    peers = lax.axis_size("space") * lax.axis_size("chan")
    upper = lax.axis_index("chan") % 2 == 1
    own = jnp.transpose(volume.reshape(4, 2, SIDE, SIDE), (2, 1, 0, 3)).reshape(SIDE, 8, SIDE)
    mate = lax.ppermute(own, AXES, [(i, i ^ 1) for i in range(peers)])
    low = jnp.where(upper, mate[SIDE - WINDOW :], own[:WINDOW])
    high = jnp.where(upper, own[SIDE - WINDOW :], mate[:WINDOW])
    planes = [low[:, :4], low[:, 4:], high[:, :4], high[:, 4:]]
    upward = jnp.stack(planes[1:])
    downward = jnp.stack(planes[:2] + [jnp.zeros_like(planes[0])])
    odd = lax.axis_index("chan") // 2 % 2 == 1
    ends = (0, 1, peers - 2, peers - 1)
    first_swap = lax.ppermute(jnp.where(odd, downward, upward), AXES, [(i, i ^ 2) for i in range(peers)])
    second_swap = lax.ppermute(
        jnp.where(odd, upward, downward),
        AXES,
        [(i, i ^ 1) if i in ends else (i, i + 2 if i // 2 % 2 else i - 2) for i in range(peers)],
    )
    spread, inner = spread_weights(conv1_weight)
    w2 = conv2_weight.reshape(3, 1152, 128)
    bias = jnp.stack([conv1_bias, conv2_bias])
    partial, known = local(low, high, inner, w2, bias)
    half = convolve(
        *(first_swap, second_swap, spread, w2, bias),
        jnp.asarray(pool_matrix(), jnp.bfloat16),
        partial,
        known,
    )
    moved = lax.all_to_all(half.reshape(16, 8, 512), "chan", split_axis=0, concat_axis=0, tiled=True)
    return jnp.transpose(moved.reshape(8, 2, 8, 512), (2, 0, 1, 3)).reshape(8, 8, 1024)


def solution(mesh):
    in_specs = (P(None, AXES, None), P(), P(), P(), P())
    out_specs = P("chan", "space", None)
    return jax.shard_map(shards, mesh=mesh, in_specs=in_specs, out_specs=out_specs, check_vma=False)
```

```python
import jax
import jax.numpy as jnp
import numpy as np
from jax import lax
from jax.experimental import pallas as pl
from jax.experimental.pallas import tpu as pltpu
from jax.sharding import PartitionSpec as P

SIDE = 128
AXES = ("space", "chan")
WINDOW = 68
ROWS = 34
LINE = 20
GROUP = 6
SPLIT = 2


def leaky_relu(value):
    return jnp.maximum(value, 0.2 * value)


def column(place):
    return 8 * (place % 8) + place // 8


def gathered(columns, start, rows):
    columns[start : start + 8, :] = jnp.zeros((8, 128), jnp.float32)
    columns[start + 8 : start + 136, :] = jnp.transpose(rows.astype(jnp.bfloat16)).astype(jnp.float32)
    every = [columns[pl.ds(start + 7 + k, 8, stride=16), :] for k in range(17)]
    return [jnp.concatenate([every[2 * b + tap] for b in range(8)], axis=0).astype(jnp.bfloat16) for tap in range(3)]


def widened(row):
    sublane = lax.broadcasted_iota(jnp.int32, (8, row.shape[1]), 0)
    before = jnp.where(sublane == 0, 0.0, pltpu.roll(row[56:64], 1, 0))
    after = jnp.where(sublane == 7, 0.0, pltpu.roll(row[0:8], 7, 0))
    return jnp.concatenate([before, row, after], axis=0).astype(jnp.bfloat16)


def accumulators():
    return [pltpu.ACC(unit)((64, 256), jnp.float32) for unit in range(2) for _ in range(16)]


def local_body(low, high, w1, w2, bias, out, patches, lines, columns, center, shift):
    pl.run_scoped(
        lambda *acc: compute_local(
            (acc[:16], acc[16:]), low, high, w1, w2, bias, out, patches, lines, columns, center, shift
        ),
        *accumulators(),
    )


def compute_local(acc, low, high, w1, w2, bias, out, patches, lines, columns, center, shift):
    core = lax.axis_index("chan") % 2
    lines[0:4] = jnp.zeros((4, 16, 128), jnp.float32)
    lines[68:76] = jnp.zeros((8, 16, 128), jnp.float32)
    span = pl.ds(4 - 4 * core, WINDOW)
    lines[span, 0:8] = low[...].astype(jnp.float32)
    lines[span, 8:16] = high[...].astype(jnp.float32)
    flat = lines.reshape(76 * 16, 128)

    for i in range(0, ROWS, 2):
        rows = jnp.concatenate([flat[i * 32 + 16 : i * 32 + 80], flat[i * 32 + 48 : i * 32 + 112]], axis=0)
        for tap, picked in enumerate(gathered(columns, i // 2 * 136, rows)):
            patches[i * 32 : i * 32 + 64, tap * 128 : tap * 128 + 128] = picked

    bias1 = jnp.concatenate([bias[0:1]] * 2, axis=1)
    for unit, pieces in enumerate((range(0, 9), range(9, 17))):
        for half in range(2):
            pltpu.matmul_push_rhs(w1[half * 256 : half * 256 + 256, :], half, unit)
            for n, i in enumerate(pieces):
                if half == 0:
                    lhs = patches[i * 64 : i * 64 + 64, 0:256]
                else:
                    lhs = patches[i * 64 : i * 64 + 64, 256:384]
                    lhs = jnp.concatenate([lhs, lhs], axis=1)
                pltpu.matmul_acc_lhs(acc[unit][n], lhs, half if n == 0 else None)
        for n, i in enumerate(pieces):
            row = leaky_relu(pltpu.matmul_pop(acc[unit][n]) + bias1)
            wide = widened(row)
            row = row.astype(jnp.bfloat16)
            for side in range(2):
                lanes = slice(side * 128, side * 128 + 128)
                index = 2 * i + side
                center[index * 64 : index * 64 + 64, :] = row[:, lanes]
                shift[index * 80 : index * 80 + 80, :] = wide[:, lanes]

    @pl.when(core == 0)
    def _():
        center[0:64, :] = jnp.zeros((64, 128), jnp.bfloat16)
        shift[0:80, :] = jnp.zeros((80, 128), jnp.bfloat16)

    @pl.when(core == 1)
    def _():
        center[33 * 64 : 34 * 64, :] = jnp.zeros((64, 128), jnp.bfloat16)
        shift[33 * 80 : 34 * 80, :] = jnp.zeros((80, 128), jnp.bfloat16)

    bias2 = jnp.concatenate([bias[1:2]] * 2, axis=1)
    taps = [(r, c) for r in range(3) for c in range(3)]
    for t in range(0, 9, 2):
        pair_of = (taps[t : t + 2] * 2)[:2]
        rhs = [jnp.concatenate([block_of(w2, 2, r, c), block_of(w2, 1, r, c)], axis=1) for r, c in taps[t : t + 2]]
        if len(rhs) == 1:
            rhs.append(jnp.zeros((128, 256), jnp.bfloat16))
        rhs = jnp.concatenate(rhs, axis=0)
        for unit in range(2):
            pltpu.matmul_push_rhs(rhs, t // 2 % 2, unit)
            for i in range(16):
                row = unit * 16 + i
                lhs = jnp.concatenate([places_of(center, shift, row + r, c) for r, c in pair_of], axis=1)
                pltpu.matmul_acc_lhs(acc[unit][i], lhs, t // 2 % 2 if i == 0 else None)
    for i in range(16):
        for unit in range(2):
            out[unit * 16 + i] = pltpu.matmul_pop(acc[unit][i]) + bias2


def block_of(w2, depth_tap, row_tap, tap):
    if not 0 <= row_tap < 3:
        return jnp.zeros((128, 128), jnp.bfloat16)
    at = (row_tap * 3 + tap) * 128
    return w2[depth_tap, at : at + 128]


def places_of(center, shift, row, tap):
    if tap == 1:
        return center[row * 64 : row * 64 + 64, :]
    at = row * 80 + (0 if tap == 0 else 16)
    return shift[at : at + 64, :]


def pool_matrix():
    pooled, cell = np.arange(64)[:, None], np.arange(256)[None, :]
    return pooled == cell // 128 * 32 + column(cell % 64) // 2


def body(first_swap, second_swap, w1, w2, bias, pool, partial, known, out, *scratch):
    pl.run_scoped(
        lambda *acc: compute(
            (acc[:16], acc[16:]),
            *(first_swap, second_swap, w1, w2, bias, pool, partial, known, out),
            *scratch,
        ),
        *accumulators(),
    )


def compute(
    acc,
    first_swap,
    second_swap,
    w1,
    w2,
    bias,
    pool,
    partial,
    known,
    out,
    lines,
    columns,
    patches,
    center,
    shift,
    edges,
    cells,
):
    core = lax.axis_index("chan") % 2
    pair = lax.axis_index("space") * (lax.axis_size("chan") // 2) + lax.axis_index("chan") // 2
    pairs = lax.axis_size("space") * (lax.axis_size("chan") // 2)
    odd = pair % 2 == 1

    for g in range(35):
        pieces = []
        for t in (2 * g, 2 * g + 1):
            at = t - 3 + 4 * core
            inside = (at >= 0) & (at < WINDOW)
            at = jnp.clip(at, 0, WINDOW - 1)
            for plane in range(5):
                if plane < 3:
                    keep = inside & (pair != 0)
                    x, y = first_swap[plane, at], second_swap[plane, at]
                else:
                    keep = inside
                    x, y = second_swap[plane - 3, at], first_swap[plane - 3, at]
                value = jnp.where(odd, x.astype(jnp.float32), y.astype(jnp.float32))
                pieces.append(jnp.where(keep, value, 0.0))
        lines[g * 40 : g * 40 + 40, :] = jnp.concatenate(pieces, axis=0)

    for i in range(0, ROWS, 2):
        rows = jnp.concatenate([lines[i * 40 : i * 40 + 64, :], lines[i * 40 + 40 : i * 40 + 104, :]], axis=0)
        for tap, picked in enumerate(gathered(columns, i // 2 * 136, rows)):
            patches[i * 32 : i * 32 + 64, tap * 128 : tap * 128 + 128] = picked

    @pl.when(core == 2)
    def _():
        columns[0:8, :] = jnp.zeros((8, 128), jnp.float32)

    def both(i, tile):
        at = slice(i * 64, i * 64 + 64)
        if tile == 0:
            return known[at, 0:256]
        if tile == 1:
            return jnp.concatenate([known[at, 256:384], patches[at, 0:128]], axis=1)
        return patches[at, 128:384]

    def arrived(i, tile):
        at = slice(i * 64, i * 64 + 64)
        if tile == 0:
            return patches[at, 0:256]
        return jnp.concatenate([patches[at, 256:384]] * 2, axis=1)

    bias1 = jnp.concatenate([bias[0:1]] * 2, axis=1)
    work = []
    for unit in range(2):
        jobs = [(1 + unit, 512 + 768 * unit, 3, both, range(i, min(i + GROUP, 17))) for i in range(0, 17, GROUP)]
        jobs += [(0, 0, 2, arrived, part) for part in ((range(0, 5), range(5, 9)), (range(9, 13), range(13, 17)))[unit]]
        work.append(jobs)
    for turn in range(len(work[0]) + 1):
        base = turn % 2 * 8
        if turn < len(work[0]):
            for unit in range(2):
                _, start, tiles, lhs_of, pairs_of_rows = work[unit][turn]
                for tile in range(tiles):
                    pltpu.matmul_push_rhs(w1[start + tile * 256 : start + tile * 256 + 256, :], tile % 2, unit)
                    for n, i in enumerate(pairs_of_rows):
                        pltpu.matmul_acc_lhs(acc[unit][base + n], lhs_of(i, tile), tile % 2 if n == 0 else None)
        if turn:
            for unit in range(2):
                plane, _, _, _, pairs_of_rows = work[unit][turn - 1]
                for n, i in enumerate(pairs_of_rows):
                    row = leaky_relu(pltpu.matmul_pop(acc[unit][8 - base + n]) + bias1)
                    wide = widened(row)
                    row = row.astype(jnp.bfloat16)
                    for side in range(2):
                        lanes = slice(side * 128, side * 128 + 128)
                        index = 2 * i + side
                        center[plane, index * 64 : index * 64 + 64, :] = row[:, lanes]
                        shift[plane, index * 80 : index * 80 + 80, :] = wide[:, lanes]

    @pl.when(core == 0)
    def _():
        center[:, 0:64, :] = jnp.zeros((3, 64, 128), jnp.bfloat16)
        shift[:, 0:80, :] = jnp.zeros((3, 80, 128), jnp.bfloat16)

    @pl.when(core == 1)
    def _():
        center[:, 33 * 64 : 34 * 64, :] = jnp.zeros((3, 64, 128), jnp.bfloat16)
        shift[:, 33 * 80 : 34 * 80, :] = jnp.zeros((3, 80, 128), jnp.bfloat16)

    def block(plane, row, tap):
        return places_of(center.at[plane], shift.at[plane], row, tap)

    inner = [(r, c) for r in range(3) for c in range(3)]
    outer = [(r, c) for r in range(4) for c in range(3)]
    turn = 0
    for t in range(0, 12, 2):
        for unit, (plane, depth_tap) in enumerate(((0, 0), (2, 2))):
            rhs = jnp.concatenate(
                [
                    jnp.concatenate([block_of(w2, depth_tap, r, c), block_of(w2, depth_tap, r - 1, c)], axis=1)
                    for r, c in outer[t : t + 2]
                ],
                axis=0,
            )
            pltpu.matmul_push_rhs(rhs, turn % 2, unit)
            for i in range(16):
                lhs = jnp.concatenate([block(plane, 2 * i + r, c) for r, c in outer[t : t + 2]], axis=1)
                pltpu.matmul_acc_lhs(acc[unit][i], lhs, turn % 2 if i == 0 else None)
        turn += 1
    for unit in range(2):
        for i in range(16):
            value = pltpu.matmul_pop(acc[unit][i])
            value = jnp.where(pair == (pairs - 1 if unit else 0), 0.0, value)
            for side in range(2):
                lanes = slice(unit * 128, unit * 128 + 128)
                edges[2 * i + side, :, lanes] = (
                    value[:, side * 128 : side * 128 + 128] + partial[2 * i + side, :, lanes]
                )

    def active(rows):
        for i in rows:
            for unit in range(2):
                value = leaky_relu(pltpu.matmul_pop(acc[unit][i]) + edges[unit * 16 + i])
                at = (unit * 16 + i) * 64
                cells[at : at + 64, :] = value.astype(jnp.bfloat16)

    def pooled(quarters):
        for k in quarters:
            for unit in range(2):
                at = (unit * 4 + k) * 256
                pltpu.matmul_push_rhs(cells[at : at + 256, :], k % 2, unit)
                pltpu.matmul_acc_lhs(acc[unit][k], pool[...], k % 2)
        for k in quarters[::2]:
            for unit in range(2):
                sums = jnp.concatenate([pltpu.matmul_pop(acc[unit][k + n]) for n in range(2)], axis=0)
                mean = (sums[:, :128] + sums[:, 128:]) * 0.125
                at = unit * 256 + k * 64
                out[:, at : at + 128] = jnp.transpose(mean).astype(jnp.bfloat16)

    for m in range(SPLIT):
        rows = 16 // SPLIT
        for t in range(0, 9, 2):
            pair_of = (inner[t : t + 2] * 2)[:2]
            rhs = [
                jnp.concatenate([block_of(w2, 1, r, c), block_of(w2, 0, r, c)], axis=1) for r, c in inner[t : t + 2]
            ]
            if len(rhs) == 1:
                rhs.append(jnp.zeros((128, 256), jnp.bfloat16))
            rhs = jnp.concatenate(rhs, axis=0)
            for unit in range(2):
                pltpu.matmul_push_rhs(rhs, turn % 2, unit)
                for i in range(rows):
                    row = unit * 16 + m * rows + i
                    lhs = jnp.concatenate([block(1, row + r, c) for r, c in pair_of], axis=1)
                    pltpu.matmul_acc_lhs(acc[unit][m * rows + i], lhs, turn % 2 if i == 0 else None)
            turn += 1
        active(range(m * rows, m * rows + rows))
    pooled(range(4))


def call(body, out, scratch, flops, *operands):
    vmem = pl.BlockSpec(memory_space=pltpu.VMEM)
    return pl.pallas_call(
        body,
        out_shape=[jax.ShapeDtypeStruct(*shape) for shape in out],
        in_specs=[vmem] * len(operands),
        out_specs=[vmem] * len(out),
        scratch_shapes=[pltpu.VMEM(*shape) for shape in scratch],
        compiler_params=pltpu.CompilerParams(vmem_limit_bytes=24 << 20),
        cost_estimate=pl.CostEstimate(flops=flops, bytes_accessed=4_000_000, transcendentals=0),
    )(*operands)


def local(*operands):
    out = [((32, 64, 256), jnp.float32), ((ROWS * 32, 384), jnp.bfloat16)]
    scratch = [
        ((76, 16, 128), jnp.float32),
        ((ROWS // 2 * 136, 128), jnp.float32),
        ((ROWS * 64, 128), jnp.bfloat16),
        ((ROWS * 80, 128), jnp.bfloat16),
    ]
    return call(local_body, out, scratch, 2_000_000_000, *operands)


def convolve(*operands):
    scratch = [
        ((35 * 2 * LINE, 128), jnp.float32),
        ((ROWS // 2 * 136, 128), jnp.float32),
        ((ROWS * 32, 384), jnp.bfloat16),
        ((3, ROWS * 64, 128), jnp.bfloat16),
        ((3, ROWS * 80, 128), jnp.bfloat16),
        ((32, 64, 256), jnp.float32),
        ((2048, 256), jnp.bfloat16),
    ]
    return call(body, [((128, 512), jnp.bfloat16)], scratch, 8_000_000_000, *operands)[0]


def spread_weights(weight):
    channels = weight.shape[4]
    taps = jnp.transpose(weight, (2, 1, 0, 3, 4)).reshape(3, 3, 12, channels)

    def paired(value, before, after):
        value = jnp.pad(value, ((0, 0), (0, 0), (before, after), (0, 0)))
        value = value.reshape(3, -1, channels)
        value = jnp.pad(value, ((0, 0), (0, 64 - value.shape[1]), (0, 0)))
        sides = [jnp.pad(value, ((0, 0), (0, 0), (0, channels))), jnp.pad(value, ((0, 0), (0, 0), (channels, 0)))]
        return jnp.stack(sides, axis=1).reshape(384, 2 * channels)

    nothing = jnp.zeros((128, 2 * channels), weight.dtype)
    inner = jnp.concatenate([paired(taps, 4, 0), nothing])
    first, rest = taps[:, :, :4], taps[:, :, 4:]
    others = [paired(taps, 0, 8), nothing]
    others += [paired(rest, 0, 8), paired(first, 8, 8)]
    others += [paired(first, 12, 0), paired(rest, 12, 0)]
    return jnp.concatenate(others), inner


def shards(volume, conv1_weight, conv1_bias, conv2_weight, conv2_bias):
    peers = lax.axis_size("space") * lax.axis_size("chan")
    upper = lax.axis_index("chan") % 2 == 1
    own = jnp.transpose(volume.reshape(4, 2, SIDE, SIDE), (2, 1, 0, 3)).reshape(SIDE, 8, SIDE)
    mate = lax.ppermute(own, AXES, [(i, i ^ 1) for i in range(peers)])
    low = jnp.where(upper, mate[SIDE - WINDOW :], own[:WINDOW])
    high = jnp.where(upper, own[SIDE - WINDOW :], mate[:WINDOW])
    planes = [low[:, :4], low[:, 4:], high[:, :4], high[:, 4:]]
    upward = jnp.stack(planes[1:])
    downward = jnp.stack(planes[:2] + [jnp.zeros_like(planes[0])])
    odd = lax.axis_index("chan") // 2 % 2 == 1
    ends = (0, 1, peers - 2, peers - 1)
    one, two = jnp.where(odd, downward, upward), jnp.where(odd, upward, downward)
    one, two, conv1_weight = lax.optimization_barrier((one, two, conv1_weight))
    first_swap = lax.ppermute(one, AXES, [(i, i ^ 2) for i in range(peers)])
    second_swap = lax.ppermute(
        two,
        AXES,
        [(i, i ^ 1) if i in ends else (i, i + 2 if i // 2 % 2 else i - 2) for i in range(peers)],
    )
    spread, inner = spread_weights(conv1_weight)
    w2 = conv2_weight.reshape(3, 1152, 128)
    bias = jnp.stack([conv1_bias, conv2_bias])
    partial, known = local(low, high, inner, w2, bias)
    half = convolve(
        *(first_swap, second_swap, spread, w2, bias),
        jnp.asarray(pool_matrix(), jnp.bfloat16),
        partial,
        known,
    )
    moved = lax.all_to_all(half.reshape(16, 8, 512), "chan", split_axis=0, concat_axis=0, tiled=True)
    return jnp.transpose(moved.reshape(8, 2, 8, 512), (2, 0, 1, 3)).reshape(8, 8, 1024)


def solution(mesh):
    in_specs = (P(None, AXES, None), P(), P(), P(), P())
    out_specs = P("chan", "space", None)
    return jax.shard_map(shards, mesh=mesh, in_specs=in_specs, out_specs=out_specs, check_vma=False)
```

```python
import jax
import jax.numpy as jnp
import numpy as np
from jax import lax
from jax.experimental import pallas as pl
from jax.experimental.pallas import tpu as pltpu
from jax.sharding import PartitionSpec as P

SIDE = 128
AXES = ("space", "chan")
WINDOW = 68
ROWS = 34
LINE = 20
GROUP = 6
SPLIT = 2


def leaky_relu(value):
    return jnp.maximum(value, 0.2 * value)


def column(place):
    return 8 * (place % 8) + place // 8


def gathered(columns, start, rows):
    columns[start : start + 8, :] = jnp.zeros((8, 128), jnp.float32)
    columns[start + 8 : start + 136, :] = jnp.transpose(rows.astype(jnp.bfloat16)).astype(jnp.float32)
    every = [columns[pl.ds(start + 7 + k, 8, stride=16), :] for k in range(17)]
    return [jnp.concatenate([every[2 * b + tap] for b in range(8)], axis=0).astype(jnp.bfloat16) for tap in range(3)]


def widened(row):
    sublane = lax.broadcasted_iota(jnp.int32, (8, row.shape[1]), 0)
    before = jnp.where(sublane == 0, 0.0, pltpu.roll(row[56:64], 1, 0))
    after = jnp.where(sublane == 7, 0.0, pltpu.roll(row[0:8], 7, 0))
    return jnp.concatenate([before, row, after], axis=0).astype(jnp.bfloat16)


def accumulators():
    return [pltpu.ACC(unit)((64, 256), jnp.float32) for unit in range(2) for _ in range(16)]


def local_body(low, high, w1, w2, bias, out, patches, lines, columns, center, shift):
    pl.run_scoped(
        lambda *acc: compute_local(
            (acc[:16], acc[16:]), low, high, w1, w2, bias, out, patches, lines, columns, center, shift
        ),
        *accumulators(),
    )


def compute_local(acc, low, high, w1, w2, bias, out, patches, lines, columns, center, shift):
    core = lax.axis_index("chan") % 2
    lines[0:4] = jnp.zeros((4, 16, 128), jnp.float32)
    lines[68:76] = jnp.zeros((8, 16, 128), jnp.float32)
    span = pl.ds(4 - 4 * core, WINDOW)
    lines[span, 0:8] = low[...].astype(jnp.float32)
    lines[span, 8:16] = high[...].astype(jnp.float32)
    flat = lines.reshape(76 * 16, 128)

    for i in range(0, ROWS, 2):
        rows = jnp.concatenate([flat[i * 32 + 16 : i * 32 + 80], flat[i * 32 + 48 : i * 32 + 112]], axis=0)
        for tap, picked in enumerate(gathered(columns, i // 2 * 136, rows)):
            patches[i * 32 : i * 32 + 64, tap * 128 : tap * 128 + 128] = picked

    bias1 = jnp.concatenate([bias[0:1]] * 2, axis=1)
    for unit, pieces in enumerate((range(0, 9), range(9, 17))):
        for half in range(2):
            pltpu.matmul_push_rhs(w1[half * 256 : half * 256 + 256, :], half, unit)
            for n, i in enumerate(pieces):
                if half == 0:
                    lhs = patches[i * 64 : i * 64 + 64, 0:256]
                else:
                    lhs = patches[i * 64 : i * 64 + 64, 256:384]
                    lhs = jnp.concatenate([lhs, lhs], axis=1)
                pltpu.matmul_acc_lhs(acc[unit][n], lhs, half if n == 0 else None)
        for n, i in enumerate(pieces):
            row = leaky_relu(pltpu.matmul_pop(acc[unit][n]) + bias1)
            wide = widened(row)
            row = row.astype(jnp.bfloat16)
            for side in range(2):
                lanes = slice(side * 128, side * 128 + 128)
                index = 2 * i + side
                center[index * 64 : index * 64 + 64, :] = row[:, lanes]
                shift[index * 80 : index * 80 + 80, :] = wide[:, lanes]

    @pl.when(core == 0)
    def _():
        center[0:64, :] = jnp.zeros((64, 128), jnp.bfloat16)
        shift[0:80, :] = jnp.zeros((80, 128), jnp.bfloat16)

    @pl.when(core == 1)
    def _():
        center[33 * 64 : 34 * 64, :] = jnp.zeros((64, 128), jnp.bfloat16)
        shift[33 * 80 : 34 * 80, :] = jnp.zeros((80, 128), jnp.bfloat16)

    bias2 = jnp.concatenate([bias[1:2]] * 2, axis=1)
    taps = [(r, c) for r in range(3) for c in range(3)]
    for t in range(0, 9, 2):
        pair_of = (taps[t : t + 2] * 2)[:2]
        rhs = [jnp.concatenate([block_of(w2, 2, r, c), block_of(w2, 1, r, c)], axis=1) for r, c in taps[t : t + 2]]
        if len(rhs) == 1:
            rhs.append(jnp.zeros((128, 256), jnp.bfloat16))
        rhs = jnp.concatenate(rhs, axis=0)
        for unit in range(2):
            pltpu.matmul_push_rhs(rhs, t // 2 % 2, unit)
            for i in range(16):
                row = unit * 16 + i
                lhs = jnp.concatenate([places_of(center, shift, row + r, c) for r, c in pair_of], axis=1)
                pltpu.matmul_acc_lhs(acc[unit][i], lhs, t // 2 % 2 if i == 0 else None)
    for i in range(16):
        for unit in range(2):
            out[unit * 16 + i] = pltpu.matmul_pop(acc[unit][i]) + bias2


def block_of(w2, depth_tap, row_tap, tap):
    if not 0 <= row_tap < 3:
        return jnp.zeros((128, 128), jnp.bfloat16)
    at = (row_tap * 3 + tap) * 128
    return w2[depth_tap, at : at + 128]


def places_of(center, shift, row, tap):
    if tap == 1:
        return center[row * 64 : row * 64 + 64, :]
    at = row * 80 + (0 if tap == 0 else 16)
    return shift[at : at + 64, :]


def pool_matrix():
    pooled, cell = np.arange(64)[:, None], np.arange(256)[None, :]
    return pooled == cell // 128 * 32 + column(cell % 64) // 2


def body(first_swap, second_swap, w1, w2, bias, pool, partial, known, out, *scratch):
    pl.run_scoped(
        lambda *acc: compute(
            (acc[:16], acc[16:]),
            *(first_swap, second_swap, w1, w2, bias, pool, partial, known, out),
            *scratch,
        ),
        *accumulators(),
    )


def compute(
    acc,
    first_swap,
    second_swap,
    w1,
    w2,
    bias,
    pool,
    partial,
    known,
    out,
    lines,
    columns,
    patches,
    center,
    shift,
    edges,
    cells,
):
    core = lax.axis_index("chan") % 2
    pair = lax.axis_index("space") * (lax.axis_size("chan") // 2) + lax.axis_index("chan") // 2
    pairs = lax.axis_size("space") * (lax.axis_size("chan") // 2)
    odd = pair % 2 == 1

    for g in range(35):
        pieces = []
        for t in (2 * g, 2 * g + 1):
            at = t - 3 + 4 * core
            inside = (at >= 0) & (at < WINDOW)
            at = jnp.clip(at, 0, WINDOW - 1)
            for plane in range(5):
                if plane < 3:
                    keep = inside & (pair != 0)
                    x, y = first_swap[plane, at], second_swap[plane, at]
                else:
                    keep = inside
                    x, y = second_swap[plane - 3, at], first_swap[plane - 3, at]
                value = jnp.where(odd, x.astype(jnp.float32), y.astype(jnp.float32))
                pieces.append(jnp.where(keep, value, 0.0))
        lines[g * 40 : g * 40 + 40, :] = jnp.concatenate(pieces, axis=0)

    for i in range(0, ROWS, 2):
        rows = jnp.concatenate([lines[i * 40 : i * 40 + 64, :], lines[i * 40 + 40 : i * 40 + 104, :]], axis=0)
        for tap, picked in enumerate(gathered(columns, i // 2 * 136, rows)):
            patches[i * 32 : i * 32 + 64, tap * 128 : tap * 128 + 128] = picked

    @pl.when(core == 2)
    def _():
        columns[0:8, :] = jnp.zeros((8, 128), jnp.float32)

    def both(i, tile):
        at = slice(i * 64, i * 64 + 64)
        if tile == 0:
            return known[at, 0:256]
        if tile == 1:
            return jnp.concatenate([known[at, 256:384], patches[at, 0:128]], axis=1)
        return patches[at, 128:384]

    def arrived(i, tile):
        at = slice(i * 64, i * 64 + 64)
        if tile == 0:
            return patches[at, 0:256]
        return jnp.concatenate([patches[at, 256:384]] * 2, axis=1)

    bias1 = jnp.concatenate([bias[0:1]] * 2, axis=1)
    work = []
    for unit in range(2):
        jobs = [(1 + unit, 512 + 768 * unit, 3, both, range(i, min(i + GROUP, 17))) for i in range(0, 17, GROUP)]
        jobs += [(0, 0, 2, arrived, part) for part in ((range(0, 5), range(5, 9)), (range(9, 13), range(13, 17)))[unit]]
        work.append(jobs)
    for turn in range(len(work[0]) + 1):
        base = turn % 2 * 8
        if turn < len(work[0]):
            for unit in range(2):
                _, start, tiles, lhs_of, pairs_of_rows = work[unit][turn]
                for tile in range(tiles):
                    pltpu.matmul_push_rhs(w1[start + tile * 256 : start + tile * 256 + 256, :], tile % 2, unit)
                    for n, i in enumerate(pairs_of_rows):
                        pltpu.matmul_acc_lhs(acc[unit][base + n], lhs_of(i, tile), tile % 2 if n == 0 else None)
        if turn:
            for unit in range(2):
                plane, _, _, _, pairs_of_rows = work[unit][turn - 1]
                for n, i in enumerate(pairs_of_rows):
                    row = leaky_relu(pltpu.matmul_pop(acc[unit][8 - base + n]) + bias1)
                    wide = widened(row)
                    row = row.astype(jnp.bfloat16)
                    for side in range(2):
                        lanes = slice(side * 128, side * 128 + 128)
                        index = 2 * i + side
                        center[plane, index * 64 : index * 64 + 64, :] = row[:, lanes]
                        shift[plane, index * 80 : index * 80 + 80, :] = wide[:, lanes]

    @pl.when(core == 0)
    def _():
        center[:, 0:64, :] = jnp.zeros((3, 64, 128), jnp.bfloat16)
        shift[:, 0:80, :] = jnp.zeros((3, 80, 128), jnp.bfloat16)

    @pl.when(core == 1)
    def _():
        center[:, 33 * 64 : 34 * 64, :] = jnp.zeros((3, 64, 128), jnp.bfloat16)
        shift[:, 33 * 80 : 34 * 80, :] = jnp.zeros((3, 80, 128), jnp.bfloat16)

    def block(plane, row, tap):
        return places_of(center.at[plane], shift.at[plane], row, tap)

    inner = [(r, c) for r in range(3) for c in range(3)]
    outer = [(r, c) for r in range(4) for c in range(3)]
    turn = 0
    for t in range(0, 12, 2):
        for unit, (plane, depth_tap) in enumerate(((0, 0), (2, 2))):
            rhs = jnp.concatenate(
                [
                    jnp.concatenate([block_of(w2, depth_tap, r, c), block_of(w2, depth_tap, r - 1, c)], axis=1)
                    for r, c in outer[t : t + 2]
                ],
                axis=0,
            )
            pltpu.matmul_push_rhs(rhs, turn % 2, unit)
            for i in range(16):
                lhs = jnp.concatenate([block(plane, 2 * i + r, c) for r, c in outer[t : t + 2]], axis=1)
                pltpu.matmul_acc_lhs(acc[unit][i], lhs, turn % 2 if i == 0 else None)
        turn += 1
    for unit in range(2):
        for i in range(16):
            value = pltpu.matmul_pop(acc[unit][i])
            value = jnp.where(pair == (pairs - 1 if unit else 0), 0.0, value)
            for side in range(2):
                lanes = slice(unit * 128, unit * 128 + 128)
                edges[2 * i + side, :, lanes] = (
                    value[:, side * 128 : side * 128 + 128] + partial[2 * i + side, :, lanes]
                )

    def active(rows):
        for i in rows:
            for unit in range(2):
                value = leaky_relu(pltpu.matmul_pop(acc[unit][i]) + edges[unit * 16 + i])
                at = (unit * 16 + i) * 64
                cells[at : at + 64, :] = value.astype(jnp.bfloat16)

    def pooled(quarters):
        for k in quarters:
            for unit in range(2):
                at = (unit * 4 + k) * 256
                pltpu.matmul_push_rhs(cells[at : at + 256, :], k % 2, unit)
                pltpu.matmul_acc_lhs(acc[unit][k], pool[...], k % 2)
        for k in quarters[::2]:
            for unit in range(2):
                sums = jnp.concatenate([pltpu.matmul_pop(acc[unit][k + n]) for n in range(2)], axis=0)
                mean = (sums[:, :128] + sums[:, 128:]) * 0.125
                at = unit * 256 + k * 64
                out[:, at : at + 128] = jnp.transpose(mean).astype(jnp.bfloat16)

    for m in range(SPLIT):
        rows = 16 // SPLIT
        for t in range(0, 9, 2):
            pair_of = (inner[t : t + 2] * 2)[:2]
            rhs = [
                jnp.concatenate([block_of(w2, 1, r, c), block_of(w2, 0, r, c)], axis=1) for r, c in inner[t : t + 2]
            ]
            if len(rhs) == 1:
                rhs.append(jnp.zeros((128, 256), jnp.bfloat16))
            rhs = jnp.concatenate(rhs, axis=0)
            for unit in range(2):
                pltpu.matmul_push_rhs(rhs, turn % 2, unit)
                for i in range(rows):
                    row = unit * 16 + m * rows + i
                    lhs = jnp.concatenate([block(1, row + r, c) for r, c in pair_of], axis=1)
                    pltpu.matmul_acc_lhs(acc[unit][m * rows + i], lhs, turn % 2 if i == 0 else None)
            turn += 1
        active(range(m * rows, m * rows + rows))
    pooled(range(4))


def call(body, out, scratch, flops, *operands):
    vmem = pl.BlockSpec(memory_space=pltpu.VMEM)
    return pl.pallas_call(
        body,
        out_shape=[jax.ShapeDtypeStruct(*shape) for shape in out],
        in_specs=[vmem] * len(operands),
        out_specs=[vmem] * len(out),
        scratch_shapes=[pltpu.VMEM(*shape) for shape in scratch],
        compiler_params=pltpu.CompilerParams(vmem_limit_bytes=24 << 20),
        cost_estimate=pl.CostEstimate(flops=flops, bytes_accessed=4_000_000, transcendentals=0),
    )(*operands)


def local(*operands):
    out = [((32, 64, 256), jnp.float32), ((ROWS * 32, 384), jnp.bfloat16)]
    scratch = [
        ((76, 16, 128), jnp.float32),
        ((ROWS // 2 * 136, 128), jnp.float32),
        ((ROWS * 64, 128), jnp.bfloat16),
        ((ROWS * 80, 128), jnp.bfloat16),
    ]
    return call(local_body, out, scratch, 2_000_000_000, *operands)


def convolve(*operands):
    scratch = [
        ((35 * 2 * LINE, 128), jnp.float32),
        ((ROWS // 2 * 136, 128), jnp.float32),
        ((ROWS * 32, 384), jnp.bfloat16),
        ((3, ROWS * 64, 128), jnp.bfloat16),
        ((3, ROWS * 80, 128), jnp.bfloat16),
        ((32, 64, 256), jnp.float32),
        ((2048, 256), jnp.bfloat16),
    ]
    return call(body, [((128, 512), jnp.bfloat16)], scratch, 8_000_000_000, *operands)[0]


def spread_weights(weight):
    channels = weight.shape[4]
    taps = jnp.transpose(weight, (2, 1, 0, 3, 4)).reshape(3, 3, 12, channels)

    def paired(value, before, after):
        value = jnp.pad(value, ((0, 0), (0, 0), (before, after), (0, 0)))
        value = value.reshape(3, -1, channels)
        value = jnp.pad(value, ((0, 0), (0, 64 - value.shape[1]), (0, 0)))
        sides = [jnp.pad(value, ((0, 0), (0, 0), (0, channels))), jnp.pad(value, ((0, 0), (0, 0), (channels, 0)))]
        return jnp.stack(sides, axis=1).reshape(384, 2 * channels)

    nothing = jnp.zeros((128, 2 * channels), weight.dtype)
    inner = jnp.concatenate([paired(taps, 4, 0), nothing])
    first, rest = taps[:, :, :4], taps[:, :, 4:]
    others = [paired(taps, 0, 8), nothing]
    others += [paired(rest, 0, 8), paired(first, 8, 8)]
    others += [paired(first, 12, 0), paired(rest, 12, 0)]
    return jnp.concatenate(others), inner


def shards(volume, conv1_weight, conv1_bias, conv2_weight, conv2_bias):
    peers = lax.axis_size("space") * lax.axis_size("chan")
    upper = lax.axis_index("chan") % 2 == 1
    own = jnp.transpose(volume.reshape(4, 2, SIDE, SIDE), (2, 1, 0, 3)).reshape(SIDE, 8, SIDE)
    first_rows, last_rows = own[:WINDOW], own[SIDE - WINDOW :]
    mine = jnp.where(upper, last_rows, first_rows)
    mate = lax.ppermute(jnp.where(upper, first_rows, last_rows), AXES, [(i, i ^ 1) for i in range(peers)])
    low = jnp.where(upper, mate, mine)
    high = jnp.where(upper, mine, mate)
    planes = [low[:, :4], low[:, 4:], high[:, :4], high[:, 4:]]
    upward = jnp.stack(planes[1:])
    downward = jnp.stack(planes[:2] + [jnp.zeros_like(planes[0])])
    odd = lax.axis_index("chan") // 2 % 2 == 1
    ends = (0, 1, peers - 2, peers - 1)
    one, two = jnp.where(odd, downward, upward), jnp.where(odd, upward, downward)
    one, two, conv1_weight = lax.optimization_barrier((one, two, conv1_weight))
    first_swap = lax.ppermute(one, AXES, [(i, i ^ 2) for i in range(peers)])
    second_swap = lax.ppermute(
        two,
        AXES,
        [(i, i ^ 1) if i in ends else (i, i + 2 if i // 2 % 2 else i - 2) for i in range(peers)],
    )
    spread, inner = spread_weights(conv1_weight)
    w2 = conv2_weight.reshape(3, 1152, 128)
    bias = jnp.stack([conv1_bias, conv2_bias])
    partial, known = local(low, high, inner, w2, bias)
    half = convolve(
        *(first_swap, second_swap, spread, w2, bias),
        jnp.asarray(pool_matrix(), jnp.bfloat16),
        partial,
        known,
    )
    moved = lax.all_to_all(half.reshape(16, 8, 512), "chan", split_axis=0, concat_axis=0, tiled=True)
    return jnp.transpose(moved.reshape(8, 2, 8, 512), (2, 0, 1, 3)).reshape(8, 8, 1024)


def solution(mesh):
    in_specs = (P(None, AXES, None), P(), P(), P(), P())
    out_specs = P("chan", "space", None)
    return jax.shard_map(shards, mesh=mesh, in_specs=in_specs, out_specs=out_specs, check_vma=False)
```
